128 devices in a mesh: slab: 8 (over x, core), seq: 16 (over z, y).
Axes of the slice: x: 4, y: 4, z: 4, core: 2. Of those that a mesh axis runs over, the one named last changes fastest.
Arguments:
- query: bfloat16 [65536, 1024], P(('slab', 'seq')), may hold values from -6 to 6
- key: bfloat16 [65536, 1024], P(('slab', 'seq')), may hold values from -6 to 6
- value: bfloat16 [65536, 1024], P(('slab', 'seq')), may hold values from -6 to 6
- grad_out: bfloat16 [65536, 1024], P(('slab', 'seq')), may hold values from -6 to 6
- pattern: int32 [1024, 8], P('slab'), may hold values from 0 to 159, as said below
- valid_rows: int32 [1024], replicated, may hold values from 16 to 64
Outputs:
- attn_out: bfloat16 [65536, 1024], P(('slab', 'seq'))
- grad_query: bfloat16 [65536, 1024], P(('slab', 'seq'))
- grad_key: bfloat16 [65536, 1024], P(('slab', 'seq'))
- grad_value: bfloat16 [65536, 1024], P(('slab', 'seq'))
The draws below stay inside these ranges and needn't reach their ends.
Inputs may be any that keep to these rules, and one draw needn't show every extreme that they name: `pattern`: row b lists 8 different numbers; its first entry is 16 + b % 128, the block itself; every target lies in 0 to 1023.
All inputs are finite; a program needn't handle non-finite values.
Results may differ from the reference program's by a relative error of at most 0.019.
Values may be sent and summed in bfloat16 or wider, within the bound.
No kernel may reach another device: no remote copies, remote signals or barrier semaphores. Data moves between devices by JAX's collectives and lax.ppermute only.
A program may use at most 128 MiB of HBM per device.

```python
import jax
import jax.numpy as jnp
from jax import lax

HEADS = 16
HEAD_DIM = 64
D = 1024
BLOCK = 64
KEYS = 8
FACE = 16
TOKENS = 65536
QBLOCKS = 128
ALL_BLOCKS = 1024
EXT_BLOCKS = 160
N_SLAB = 8


def base_draw(key):
    return jnp.clip(jax.random.normal(key, (TOKENS, D), jnp.float32), -6.0, 6.0)


def draw_query(key, part):
    base = base_draw(jax.random.fold_in(key, 1))
    return base.astype(jnp.bfloat16)


def draw_key(key, part):
    base = base_draw(jax.random.fold_in(key, 2))
    return base.astype(jnp.bfloat16)


def draw_pattern(key, part):
    block_ids = jnp.arange(ALL_BLOCKS)
    own_slot = FACE + block_ids % QBLOCKS
    reach = jnp.arange(EXT_BLOCKS)
    noise = jax.random.randint(jax.random.fold_in(key, 21), (ALL_BLOCKS, EXT_BLOCKS), 0, 2 ** 20)
    scores = noise * EXT_BLOCKS + reach[None, :]
    barred = reach[None, :] == own_slot[:, None]
    barred = barred | (block_ids[:, None] < QBLOCKS) & (reach[None, :] < FACE)
    barred = barred | (block_ids[:, None] >= ALL_BLOCKS - QBLOCKS) & (reach[None, :] >= FACE + QBLOCKS)
    scores = jnp.where(barred, scores + 2 ** 30, scores)
    order = jnp.argsort(scores, axis=1, stable=True)
    return jnp.concatenate([own_slot[:, None], order[:, :KEYS - 1]], axis=1).astype(jnp.int32)


def draw_valid_rows(key, part):
    raw = jax.random.randint(jax.random.fold_in(key, 31), (ALL_BLOCKS,), BLOCK // 4, BLOCK + BLOCK // 2 + 1)
    counts = jnp.minimum(raw, BLOCK)
    return counts.at[0].set(BLOCK).astype(jnp.int32)


def steps_of(stream_key, dims, split, smallest, top_value):
    level, own = 1.0, jax.random.fold_in(stream_key, 6)
    for dim, parts in split:
        heights = jnp.exp(jax.random.uniform(jax.random.fold_in(own, dim), (parts,), jnp.float32, smallest / len(split), top_value / len(split)))
        level = level * jnp.repeat(heights, dims[dim] // parts).reshape([-1 if axis == dim else 1 for axis in range(len(dims))])
    return level


def normal_values(own_key, dims, deviation, most, shards=(), kind=jnp.bfloat16):
    values = jax.random.normal(own_key, dims, jnp.float32) * deviation
    if len(shards) > 0:
        values = steps_of(own_key, dims, shards, -0.22, 0.18) * values
    return jnp.clip(values, min=-most, max=most).astype(kind)


def setup_inputs(seed: int = 0) -> dict:
    streams_of = jax.random.split(jax.random.key(seed), 7)
    return {
        "query": draw_query(jax.random.fold_in(streams_of[6], 71), 0),
        "key": draw_key(jax.random.fold_in(streams_of[6], 71), 0),
        "value": normal_values(streams_of[2], (TOKENS, D), 1.0, 6.0, ((0, 128),)),
        "grad_out": normal_values(streams_of[3], (TOKENS, D), 1.0, 6.0, ((0, 128),)),
        "pattern": draw_pattern(jax.random.fold_in(streams_of[6], 71), 0),
        "valid_rows": draw_valid_rows(jax.random.fold_in(streams_of[6], 71), 0),
    }


score_scale = 0.125


def slab_pass(q_blk, g_blk, key_all, value_all, valid_rows, slot_ids):
    k_blk = key_all[slot_ids].astype(jnp.float32)
    v_blk = value_all[slot_ids].astype(jnp.float32)
    q_full = q_blk.astype(jnp.float32)
    g_full = g_blk.astype(jnp.float32)
    is_live = (jnp.arange(BLOCK)[None, None, :] < valid_rows[slot_ids][:, :, None])[:, None, :, :]
    scores = jnp.einsum("qad,qkbd->qakb", q_full, k_blk) * score_scale
    row_top = jnp.max(jnp.where(is_live, scores, -jnp.inf), axis=(2, 3), keepdims=True)
    weight = jnp.where(is_live, jnp.exp(scores - row_top), 0.0)
    totals = jnp.sum(weight, axis=(2, 3), keepdims=True)
    prob_b = (weight / totals).astype(jnp.bfloat16)
    prob_full = prob_b.astype(jnp.float32)
    out_blk = jnp.einsum("qakb,qkbd->qad", prob_full, v_blk).astype(jnp.bfloat16)
    delta_row = jnp.sum(g_full * out_blk.astype(jnp.float32), axis=-1)[:, :, None, None]
    grad_prob = jnp.einsum("qad,qkbd->qakb", g_full, v_blk)
    dscore = (prob_full * (grad_prob - delta_row)).astype(jnp.bfloat16).astype(jnp.float32)
    dq_blk = (score_scale * jnp.einsum("qakb,qkbd->qad", dscore, k_blk)).astype(jnp.bfloat16)
    dk_tile = score_scale * jnp.einsum("qakb,qad->qkbd", dscore, q_full)
    dv_tile = jnp.einsum("qakb,qad->qkbd", prob_full, g_full)
    return out_blk, dq_blk, dk_tile, dv_tile


def reference(query, key, value, grad_out, pattern, valid_rows):
    all_blocks = TOKENS // BLOCK
    block_ids = jnp.arange(all_blocks, dtype=jnp.int32)
    targets = (((block_ids // QBLOCKS) * QBLOCKS)[:, None] + pattern - FACE).astype(jnp.int32)

    def split_heads(array):
        return jnp.moveaxis(array.reshape(all_blocks, BLOCK, HEADS, HEAD_DIM), 2, 0)

    def one_head(head_items):
        q_head, k_head, v_head, g_head = head_items

        def slab_step(carry_pair, slab_items):
            q_blk, g_blk, slot_ids = slab_items
            out_blk, dq_blk, dk_tile, dv_tile = slab_pass(q_blk, g_blk, k_head, v_head, valid_rows, slot_ids)
            dk_sum = carry_pair[0].at[slot_ids].add(dk_tile)
            dv_sum = carry_pair[1].at[slot_ids].add(dv_tile)
            return (dk_sum, dv_sum), (out_blk, dq_blk)

        zeros_acc = jnp.zeros((all_blocks, BLOCK, HEAD_DIM), jnp.float32)
        slab_items = (q_head.reshape(N_SLAB, QBLOCKS, BLOCK, HEAD_DIM),
                      g_head.reshape(N_SLAB, QBLOCKS, BLOCK, HEAD_DIM),
                      targets.reshape(N_SLAB, QBLOCKS, KEYS))
        (dk_sum, dv_sum), (out_all, dq_all) = lax.scan(slab_step, (zeros_acc, zeros_acc), slab_items)
        return (out_all.reshape(all_blocks, BLOCK, HEAD_DIM), dq_all.reshape(all_blocks, BLOCK, HEAD_DIM),
                dk_sum.astype(jnp.bfloat16), dv_sum.astype(jnp.bfloat16))

    results = lax.map(one_head, (split_heads(query), split_heads(key), split_heads(value), split_heads(grad_out)))

    def join_heads(array):
        return jnp.moveaxis(array, 0, 2).reshape(TOKENS, HEADS * HEAD_DIM)

    return join_heads(results[0]), join_heads(results[1]), join_heads(results[2]), join_heads(results[3])
```

```python
from functools import partial
import math

import jax
import jax.numpy as jnp
from jax import lax
from jax.experimental import pallas as pl
from jax.experimental.pallas import tpu as pltpu
from jax.sharding import PartitionSpec as P

HEAD_DIM = 64
BLOCK = 64
FACE = 16
PAIR = 2 * HEAD_DIM

score_scale = 0.125
exp2_scale = score_scale * math.log2(math.e)


def pack_kernel(a_ref, b_ref, out_ref):
    a, b = a_ref[...], b_ref[...]
    out_ref[0] = jnp.concatenate([a[:, :HEAD_DIM], b[:, :HEAD_DIM]], axis=1)
    out_ref[1] = jnp.concatenate([a[:, HEAD_DIM:], b[:, HEAD_DIM:]], axis=1)


def pack_heads(a, b):
    rows, cols = a.shape
    heads = cols // HEAD_DIM
    half = pl.BlockSpec((rows, PAIR), lambda i: (0, i))
    return pl.pallas_call(
        pack_kernel,
        out_shape=jax.ShapeDtypeStruct((heads, rows, PAIR), a.dtype),
        grid=(heads // 2,),
        in_specs=[half, half],
        out_specs=pl.BlockSpec((2, rows, PAIR), lambda i: (i, 0, 0)),
        name="pack_heads",
    )(a, b)


def unpack_kernel(x_ref, a_ref, b_ref):
    x, y = x_ref[0], x_ref[1]
    a_ref[...] = jnp.concatenate([x[:, :HEAD_DIM], y[:, :HEAD_DIM]], axis=1)
    b_ref[...] = jnp.concatenate([x[:, HEAD_DIM:], y[:, HEAD_DIM:]], axis=1)


def unpack_heads(x):
    heads, rows, _ = x.shape
    full = jax.ShapeDtypeStruct((rows, heads * HEAD_DIM), x.dtype)
    half = pl.BlockSpec((rows, PAIR), lambda i: (0, i))
    return pl.pallas_call(
        unpack_kernel,
        out_shape=(full, full),
        grid=(heads // 2,),
        in_specs=[pl.BlockSpec((2, rows, PAIR), lambda i: (i, 0, 0))],
        out_specs=(half, half),
        name="unpack_heads",
    )(x)


def attention_kernel(
    pattern_ref, valid_ref, start_ref, qg_ref, kv_hbm, before_hbm, after_hbm,
    od_ref, mid_ref, face_ref, rim_ref, kv_ref, acc_ref, sems, *, keys_num, unroll,
):
    step = pl.program_id(0)
    face = before_hbm.shape[0]
    own = kv_hbm.shape[0]
    blocks = qg_ref.shape[0] // BLOCK

    @pl.when(step == 0)
    def _():
        copies = [
            pltpu.make_async_copy(before_hbm, kv_ref.at[pl.ds(0, face)], sems.at[0]),
            pltpu.make_async_copy(kv_hbm, kv_ref.at[pl.ds(face, own)], sems.at[1]),
            pltpu.make_async_copy(after_hbm, kv_ref.at[pl.ds(face + own, face)], sems.at[2]),
        ]
        for copy in copies:
            copy.start()
        acc_ref[...] = jnp.zeros_like(acc_ref)
        for copy in copies:
            copy.wait()

    start = start_ref[0]
    low = lax.broadcasted_iota(jnp.int32, (BLOCK, PAIR), 1) < HEAD_DIM
    lane = lax.broadcasted_iota(jnp.int32, (1, PAIR), 1)

    def one_block(i, _):
        rows = pl.ds(pl.multiple_of(i * BLOCK, BLOCK), BLOCK)
        base = (step * blocks + i) * keys_num
        slots = [pattern_ref[base + j] for j in range(keys_num)]
        counts = [valid_ref[start + slot] for slot in slots]
        spans = [pl.ds(pl.multiple_of(slot * BLOCK, BLOCK), BLOCK) for slot in slots]
        kv = jnp.concatenate([kv_ref[span, :] for span in spans], axis=0)
        bias = jnp.concatenate(
            [
                jnp.where(
                    lane < jnp.where(lane < HEAD_DIM, counts[j], counts[j + 1] + HEAD_DIM),
                    0.0,
                    -jnp.inf,
                )
                for j in range(0, keys_num, 2)
            ],
            axis=1,
        )
        qg = qg_ref[rows, :]
        zero = jnp.zeros_like(qg)
        gq = jnp.concatenate([jnp.where(low, zero, qg), jnp.where(low, qg, zero)], axis=0)
        both = lax.dot_general(
            gq, kv, (((1,), (1,)), ((), ())), preferred_element_type=jnp.float32
        )
        grad_prob, scores = both[:BLOCK], both[BLOCK:] + bias
        top = jnp.max(scores, axis=1, keepdims=True)
        weight = jnp.exp2((scores - top) * exp2_scale)
        total = jnp.sum(weight, axis=1, keepdims=True)
        prob = (weight * (1.0 / total)).astype(jnp.bfloat16)
        prob_wide = prob.astype(jnp.float32)
        delta = jnp.sum(prob_wide * grad_prob, axis=1, keepdims=True)
        dscore = (prob_wide * (grad_prob - delta)).astype(jnp.bfloat16)
        pd = jnp.concatenate([prob, dscore], axis=0)
        od = jnp.dot(pd, kv, preferred_element_type=jnp.float32)
        od_ref[rows, :] = jnp.where(low, od[BLOCK:] * score_scale, od[:BLOCK]).astype(od_ref.dtype)
        dkv = lax.dot_general(
            pd, gq, (((0,), (0,)), ((), ())), preferred_element_type=jnp.float32
        )
        for j, span in enumerate(spans):
            acc_ref[span, :] += dkv[j * BLOCK : (j + 1) * BLOCK]
        return 0

    lax.fori_loop(0, blocks, one_block, 0, unroll=unroll)

    @pl.when(step == pl.num_programs(0) - 1)
    def _():
        def scaled(first, size):
            lanes = lax.broadcasted_iota(jnp.int32, (size, PAIR), 1) < HEAD_DIM
            tile = acc_ref[pl.ds(first, size), :]
            return jnp.where(lanes, tile * score_scale, tile)

        rim_ref[:face] = scaled(0, face).astype(rim_ref.dtype)
        rim_ref[face:] = scaled(face + own, face).astype(rim_ref.dtype)
        face_ref[:face] = scaled(face, face)
        face_ref[face:] = scaled(own, face)
        mid_ref[...] = scaled(2 * face, own - 2 * face).astype(mid_ref.dtype)


def attention(pattern, valid_rows, start, qg, kv, before, after, unroll=2):
    tokens, keys_num = qg.shape[0], pattern.shape[1]
    own, face = kv.shape[0], before.shape[0]
    rows = math.gcd(tokens, 8 * BLOCK)
    smem = pl.BlockSpec(memory_space=pltpu.SMEM)
    raw = pl.BlockSpec(memory_space=pl.ANY)
    tile = pl.BlockSpec((rows, PAIR), lambda i: (i, 0))

    def whole(size):
        return pl.BlockSpec((size, PAIR), lambda i: (0, 0))

    return pl.pallas_call(
        partial(attention_kernel, keys_num=keys_num, unroll=unroll),
        out_shape=(
            jax.ShapeDtypeStruct((tokens, PAIR), qg.dtype),
            jax.ShapeDtypeStruct((own - 2 * face, PAIR), qg.dtype),
            jax.ShapeDtypeStruct((2 * face, PAIR), jnp.float32),
            jax.ShapeDtypeStruct((2 * face, PAIR), qg.dtype),
        ),
        grid=(tokens // rows,),
        in_specs=[smem, smem, smem, tile, raw, raw, raw],
        out_specs=(tile, whole(own - 2 * face), whole(2 * face), whole(2 * face)),
        scratch_shapes=[
            pltpu.VMEM((own + 2 * face, PAIR), qg.dtype),
            pltpu.VMEM((own + 2 * face, PAIR), jnp.float32),
            pltpu.SemaphoreType.DMA((3,)),
        ],
        compiler_params=pltpu.CompilerParams(vmem_limit_bytes=40 << 20),
        name="block_attention",
    )(pattern.reshape(-1), valid_rows, start, qg, kv, before, after)


def body(query, key, value, grad_out, pattern, valid_rows):
    def exchange(x):
        return lax.all_to_all(x, "seq", split_axis=0, concat_axis=0, tiled=True)

    size = lax.axis_size("slab")
    up = [(i, i + 1) for i in range(size - 1)]
    down = [(i + 1, i) for i in range(size - 1)]
    shards, face = lax.axis_size("seq"), FACE * BLOCK
    kv = exchange(pack_heads(key, value))
    qg = exchange(pack_heads(query, grad_out))
    kv = kv.reshape(-1, PAIR)
    qg = qg.reshape(-1, PAIR)
    own = kv.shape[0]
    before = lax.ppermute(kv[own - face :], "slab", up)
    after = lax.ppermute(kv[:face], "slab", down)
    start = (lax.axis_index("slab") * pattern.shape[0] - FACE).astype(jnp.int32).reshape(1)
    od, mid, faces, rims = attention(pattern, valid_rows, start, qg, kv, before, after)
    od = exchange(od.reshape(shards, -1, PAIR))
    to_before = lax.ppermute(rims[:face], "slab", down)
    to_after = lax.ppermute(rims[face:], "slab", up)
    first = (faces[:face] + to_after.astype(jnp.float32)).astype(mid.dtype)
    last = (faces[face:] + to_before.astype(jnp.float32)).astype(mid.dtype)
    dkv = exchange(jnp.concatenate([first, mid, last], axis=0).reshape(shards, -1, PAIR))
    grad_query, attn_out = unpack_heads(od)
    grad_key, grad_value = unpack_heads(dkv)
    return (attn_out, grad_query, grad_key, grad_value)


def solution(mesh):
    rows = P(("slab", "seq"), None)
    return jax.shard_map(
        body,
        mesh=mesh,
        in_specs=(rows, rows, rows, rows, P("slab", None), P()),
        out_specs=(rows, rows, rows, rows),
        check_vma=False,
    )
```

```python
from functools import partial
import math

import jax
import jax.numpy as jnp
from jax import lax
from jax.experimental import pallas as pl
from jax.experimental.pallas import tpu as pltpu
from jax.sharding import PartitionSpec as P

HEAD_DIM = 64
BLOCK = 64
FACE = 16
PAIR = 2 * HEAD_DIM
WIDE = 4

score_scale = 0.125
exp2_scale = score_scale * math.log2(math.e)


def swap_halves(a, b):
    low = jnp.concatenate([a[:, :HEAD_DIM], b[:, :HEAD_DIM]], axis=1)
    high = jnp.concatenate([a[:, HEAD_DIM:], b[:, HEAD_DIM:]], axis=1)
    return low, high


def pack_kernel(k_ref, v_ref, q_ref, g_ref, out_ref):
    rows = k_ref.shape[0]
    for p in range(k_ref.shape[1] // PAIR):
        cols = slice(p * PAIR, (p + 1) * PAIR)
        for at, (a_ref, b_ref) in enumerate(((k_ref, v_ref), (q_ref, g_ref))):
            low, high = swap_halves(a_ref[:, cols], b_ref[:, cols])
            out_ref[2 * p, at * rows : (at + 1) * rows] = low
            out_ref[2 * p + 1, at * rows : (at + 1) * rows] = high


def pack_heads(k, v, q, g):
    rows, cols = k.shape
    width = WIDE * PAIR
    part = pl.BlockSpec((rows, width), lambda i: (0, i))
    return pl.pallas_call(
        pack_kernel,
        out_shape=jax.ShapeDtypeStruct((cols // HEAD_DIM, 2 * rows, PAIR), k.dtype),
        grid=(cols // width,),
        in_specs=[part] * 4,
        out_specs=pl.BlockSpec((2 * WIDE, 2 * rows, PAIR), lambda i: (i, 0, 0)),
        compiler_params=pltpu.CompilerParams(vmem_limit_bytes=40 << 20),
        name="pack_heads",
    )(k, v, q, g)


def unpack_kernel(x_ref, k_ref, v_ref, q_ref, o_ref):
    rows = k_ref.shape[0]
    for p in range(k_ref.shape[1] // PAIR):
        cols = slice(p * PAIR, (p + 1) * PAIR)
        for at, (a_ref, b_ref) in enumerate(((k_ref, v_ref), (q_ref, o_ref))):
            part = slice(at * rows, (at + 1) * rows)
            a_ref[:, cols], b_ref[:, cols] = swap_halves(x_ref[2 * p, part], x_ref[2 * p + 1, part])


def unpack_heads(x):
    heads, rows, _ = x.shape
    rows //= 2
    width = WIDE * PAIR
    part = pl.BlockSpec((rows, width), lambda i: (0, i))
    return pl.pallas_call(
        unpack_kernel,
        out_shape=(jax.ShapeDtypeStruct((rows, heads * HEAD_DIM), x.dtype),) * 4,
        grid=(heads * HEAD_DIM // width,),
        in_specs=[pl.BlockSpec((2 * WIDE, 2 * rows, PAIR), lambda i: (i, 0, 0))],
        out_specs=(part,) * 4,
        compiler_params=pltpu.CompilerParams(vmem_limit_bytes=40 << 20),
        name="unpack_heads",
    )(x)


def attention_kernel(
    pattern_ref, valid_ref, start_ref, x_hbm, before_hbm, after_hbm,
    z_hbm, first_ref, last_ref, down_ref, up_ref,
    kv_ref, qg_ref, acc_ref, od_ref, dkv_ref, both_ref, pd_ref, in_sems, od_sems, dkv_sems,
    *, keys_num, group, lines,
):
    shards, rows = qg_ref.shape[:2]
    edge = before_hbm.shape[0]
    each = rows // BLOCK

    def fetch(source, i):
        return pltpu.make_async_copy(source, kv_ref.at[pl.ds(i * rows, rows)], in_sems.at[i])

    copies = [fetch(x_hbm.at[t, pl.ds(0, rows)], edge + t) for t in range(shards)]
    copies += [fetch(before_hbm.at[t], t) for t in range(edge)]
    copies += [fetch(after_hbm.at[t], edge + shards + t) for t in range(edge)]
    copies += [
        pltpu.make_async_copy(x_hbm.at[:, pl.ds(rows, rows)], qg_ref, in_sems.at[len(copies)])
    ]
    for copy in copies:
        copy.start()
    acc_ref[...] = jnp.zeros_like(acc_ref)
    for copy in copies:
        copy.wait()

    start = start_ref[0]
    low = lax.broadcasted_iota(jnp.int32, (BLOCK, PAIR), 1) < HEAD_DIM
    lane = lax.broadcasted_iota(jnp.int32, (1, PAIR), 1)

    def send_od(t):
        return pltpu.make_async_copy(od_ref.at[t], z_hbm.at[t, pl.ds(rows, rows)], od_sems.at[t])

    def send_dkv(t):
        return pltpu.make_async_copy(dkv_ref.at[t], z_hbm.at[t, pl.ds(0, rows)], dkv_sems.at[t])

    def one_group(t, _):
        meta = []
        for u in range(group):
            base = (t * group + u) * keys_num
            slots = [pattern_ref[base + j] for j in range(keys_num)]
            counts = [valid_ref[start + slot] for slot in slots]
            meta.append((u // each, slice(u % each * BLOCK, (u % each + 1) * BLOCK), slots, counts))
        shard = t * (group // each)

        def gathered(slots):
            return jnp.concatenate(
                [kv_ref[pl.ds(pl.multiple_of(slot * BLOCK, BLOCK), BLOCK), :] for slot in slots],
                axis=0,
            )

        def spread(s, part):
            qg = qg_ref[shard + s, part, :]
            zero = jnp.zeros_like(qg)
            return jnp.concatenate([jnp.where(low, zero, qg), jnp.where(low, qg, zero)], axis=0)

        for u, (s, part, slots, counts) in enumerate(meta):
            both_ref[u] = lax.dot_general(
                spread(s, part), gathered(slots), (((1,), (1,)), ((), ())),
                preferred_element_type=jnp.float32,
            )
        for u, (s, part, slots, counts) in enumerate(meta):
            bias = jnp.concatenate(
                [
                    jnp.where(
                        lane < jnp.where(lane < HEAD_DIM, counts[j], counts[j + 1] + HEAD_DIM),
                        0.0,
                        -jnp.inf,
                    )
                    for j in range(0, keys_num, 2)
                ],
                axis=1,
            )
            for r in range(0, BLOCK, lines):
                scores = both_ref[u, BLOCK + r : BLOCK + r + lines, :] + bias
                top = jnp.max(scores, axis=1, keepdims=True)
                weight = jnp.exp2((scores - top) * exp2_scale)
                total = jnp.sum(weight, axis=1, keepdims=True)
                prob = (weight * (1.0 / total)).astype(jnp.bfloat16)
                prob_wide = prob.astype(jnp.float32)
                grad_prob = both_ref[u, r : r + lines, :]
                delta = jnp.sum(prob_wide * grad_prob, axis=1, keepdims=True)
                dscore = (prob_wide * (grad_prob - delta)).astype(jnp.bfloat16)
                pd_ref[u, r : r + lines, :] = prob
                pd_ref[u, BLOCK + r : BLOCK + r + lines, :] = dscore
        for u, (s, part, slots, counts) in enumerate(meta):
            od = jnp.dot(pd_ref[u], gathered(slots), preferred_element_type=jnp.float32)
            od_ref[shard + s, part, :] = jnp.where(
                low, od[BLOCK:] * score_scale, od[:BLOCK]
            ).astype(od_ref.dtype)
        for s in range(group // each):
            send_od(shard + s).start()
        for u, (s, part, slots, counts) in enumerate(meta):
            dkv = lax.dot_general(
                pd_ref[u], spread(s, part), (((0,), (0,)), ((), ())),
                preferred_element_type=jnp.float32,
            )
            for j, slot in enumerate(slots):
                span = pl.ds(pl.multiple_of(slot * BLOCK, BLOCK), BLOCK)
                acc_ref[span, :] += dkv[j * BLOCK : (j + 1) * BLOCK]
        return 0

    lax.fori_loop(0, shards * each // group, one_group, 0)

    wide_low = lax.broadcasted_iota(jnp.int32, (rows, PAIR), 1) < HEAD_DIM

    def scaled(s):
        tile = acc_ref[s * rows : (s + 1) * rows, :]
        return jnp.where(wide_low, tile * score_scale, tile)

    for s in range(edge):
        down_ref[s] = scaled(s).astype(down_ref.dtype)
        up_ref[s] = scaled(edge + shards + s).astype(up_ref.dtype)
        first_ref[s] = scaled(edge + s)
        last_ref[s] = scaled(shards + s)
    for t in range(edge, shards - edge):
        dkv_ref[t] = scaled(edge + t).astype(dkv_ref.dtype)
        send_dkv(t).start()
    for t in range(shards):
        send_od(t).wait()
    for t in range(edge, shards - edge):
        send_dkv(t).wait()


def attention(pattern, valid_rows, start, x, before, after, group=16, lines=16):
    keys_num = pattern.shape[1]
    shards, rows = x.shape[0], x.shape[1] // 2
    edge = before.shape[0]
    ext = shards + 2 * edge
    smem = pl.BlockSpec(memory_space=pltpu.SMEM)
    raw = pl.BlockSpec(memory_space=pl.ANY)
    vmem = pl.BlockSpec(memory_space=pltpu.VMEM)
    face = (edge, rows, PAIR)
    return pl.pallas_call(
        partial(attention_kernel, keys_num=keys_num, group=group, lines=lines),
        out_shape=(jax.ShapeDtypeStruct(x.shape, x.dtype),)
        + (jax.ShapeDtypeStruct(face, jnp.float32),) * 2
        + (jax.ShapeDtypeStruct(face, x.dtype),) * 2,
        in_specs=[smem, smem, smem, raw, raw, raw],
        out_specs=(raw, vmem, vmem, vmem, vmem),
        scratch_shapes=[
            pltpu.VMEM((ext * rows, PAIR), x.dtype),
            pltpu.VMEM((shards, rows, PAIR), x.dtype),
            pltpu.VMEM((ext * rows, PAIR), jnp.float32),
            pltpu.VMEM((shards, rows, PAIR), x.dtype),
            pltpu.VMEM((shards, rows, PAIR), x.dtype),
            pltpu.VMEM((group, PAIR, keys_num * BLOCK), jnp.float32),
            pltpu.VMEM((group, PAIR, keys_num * BLOCK), x.dtype),
            pltpu.SemaphoreType.DMA((ext + 1,)),
            pltpu.SemaphoreType.DMA((shards,)),
            pltpu.SemaphoreType.DMA((shards,)),
        ],
        compiler_params=pltpu.CompilerParams(vmem_limit_bytes=40 << 20),
        name="block_attention",
    )(pattern.reshape(-1), valid_rows, start, x, before, after)


def join_kernel(z_in, first_ref, last_ref, low_ref, high_ref, z_hbm, sum_ref, sems):
    edge, rows = first_ref.shape[:2]
    shards = z_hbm.shape[0]
    sum_ref[0] = (first_ref[...] + low_ref[...].astype(jnp.float32)).astype(sum_ref.dtype)
    sum_ref[1] = (last_ref[...] + high_ref[...].astype(jnp.float32)).astype(sum_ref.dtype)
    copies = [
        pltpu.make_async_copy(
            sum_ref.at[i], z_hbm.at[pl.ds(at, edge), pl.ds(0, rows)], sems.at[i]
        )
        for i, at in enumerate((0, shards - edge))
    ]
    for copy in copies:
        copy.start()
    for copy in copies:
        copy.wait()


def join_faces(z, first, last, low, high):
    raw = pl.BlockSpec(memory_space=pl.ANY)
    vmem = pl.BlockSpec(memory_space=pltpu.VMEM)
    return pl.pallas_call(
        join_kernel,
        out_shape=jax.ShapeDtypeStruct(z.shape, z.dtype),
        in_specs=[raw, vmem, vmem, vmem, vmem],
        out_specs=raw,
        scratch_shapes=[pltpu.VMEM((2, *low.shape), z.dtype), pltpu.SemaphoreType.DMA((2,))],
        input_output_aliases={0: 0},
        name="join_faces",
    )(z, first, last, low, high)


def body(query, key, value, grad_out, pattern, valid_rows):
    def exchange(x):
        return lax.all_to_all(x, "seq", split_axis=0, concat_axis=0, tiled=True)

    size = lax.axis_size("slab")
    up = [(i, i + 1) for i in range(size - 1)]
    down = [(i + 1, i) for i in range(size - 1)]
    rows = query.shape[0]
    edge = FACE * BLOCK // rows
    x = exchange(pack_heads(key, value, query, grad_out))
    before = lax.ppermute(x[x.shape[0] - edge :, :rows], "slab", up)
    after = lax.ppermute(x[:edge, :rows], "slab", down)
    start = (lax.axis_index("slab") * pattern.shape[0] - FACE).astype(jnp.int32).reshape(1)
    z, first, last, to_before, to_after = attention(pattern, valid_rows, start, x, before, after)
    high = lax.ppermute(to_before, "slab", down)
    low = lax.ppermute(to_after, "slab", up)
    z = exchange(join_faces(z, first, last, low, high))
    grad_key, grad_value, grad_query, attn_out = unpack_heads(z)
    return (attn_out, grad_query, grad_key, grad_value)


def solution(mesh):
    rows = P(("slab", "seq"), None)
    return jax.shard_map(
        body,
        mesh=mesh,
        in_specs=(rows, rows, rows, rows, P("slab", None), P()),
        out_specs=(rows, rows, rows, rows),
        check_vma=False,
    )
```

```python
from functools import partial
import math

import jax
import jax.numpy as jnp
from jax import lax
from jax.experimental import pallas as pl
from jax.experimental.pallas import tpu as pltpu
from jax.sharding import PartitionSpec as P

HEAD_DIM = 64
BLOCK = 64
FACE = 16
PAIR = 2 * HEAD_DIM
WIDE = 4

score_scale = 0.125
exp2_scale = score_scale * math.log2(math.e)


def on_chip(x):
    return pltpu.with_memory_space_constraint(x, pltpu.VMEM)


def off_chip(x):
    return pltpu.with_memory_space_constraint(x, pltpu.HBM)


def faces_kernel(x_hbm, first_ref, last_ref, sems):
    edge, rows = first_ref.shape[:2]
    copies = [
        pltpu.make_async_copy(x_hbm.at[pl.ds(at, edge), pl.ds(0, rows)], ref, sems.at[i])
        for i, (at, ref) in enumerate(((0, first_ref), (x_hbm.shape[0] - edge, last_ref)))
    ]
    for copy in copies:
        copy.start()
    for copy in copies:
        copy.wait()


def take_faces(x, edge, rows):
    vmem = pl.BlockSpec(memory_space=pltpu.VMEM)
    return pl.pallas_call(
        faces_kernel,
        out_shape=(pltpu.VMEM((edge, rows, PAIR), x.dtype),) * 2,
        in_specs=[pl.BlockSpec(memory_space=pltpu.HBM)],
        out_specs=(vmem, vmem),
        scratch_shapes=[pltpu.SemaphoreType.DMA((2,))],
        compiler_params=pltpu.CompilerParams(vmem_limit_bytes=4 << 20),
        name="take_faces",
    )(off_chip(x))


def swap_halves(a, b):
    low = jnp.concatenate([a[:, :HEAD_DIM], b[:, :HEAD_DIM]], axis=1)
    high = jnp.concatenate([a[:, HEAD_DIM:], b[:, HEAD_DIM:]], axis=1)
    return low, high


def pack_kernel(k_ref, v_ref, q_ref, g_ref, out_ref):
    rows = k_ref.shape[0]
    for p in range(k_ref.shape[1] // PAIR):
        cols = slice(p * PAIR, (p + 1) * PAIR)
        for at, (a_ref, b_ref) in enumerate(((k_ref, v_ref), (q_ref, g_ref))):
            low, high = swap_halves(a_ref[:, cols], b_ref[:, cols])
            out_ref[2 * p, at * rows : (at + 1) * rows] = low
            out_ref[2 * p + 1, at * rows : (at + 1) * rows] = high


def pack_heads(k, v, q, g):
    rows, cols = k.shape
    width = WIDE * PAIR
    part = pl.BlockSpec((rows, width), lambda i: (0, i))
    return pl.pallas_call(
        pack_kernel,
        out_shape=jax.ShapeDtypeStruct((cols // HEAD_DIM, 2 * rows, PAIR), k.dtype),
        grid=(cols // width,),
        in_specs=[part] * 4,
        out_specs=pl.BlockSpec((2 * WIDE, 2 * rows, PAIR), lambda i: (i, 0, 0)),
        compiler_params=pltpu.CompilerParams(vmem_limit_bytes=60 << 20),
        name="pack_heads",
    )(k, v, q, g)


def unpack_kernel(x_ref, k_ref, v_ref, q_ref, o_ref):
    rows = k_ref.shape[0]
    for p in range(k_ref.shape[1] // PAIR):
        cols = slice(p * PAIR, (p + 1) * PAIR)
        for at, (a_ref, b_ref) in enumerate(((k_ref, v_ref), (q_ref, o_ref))):
            part = slice(at * rows, (at + 1) * rows)
            a_ref[:, cols], b_ref[:, cols] = swap_halves(x_ref[2 * p, part], x_ref[2 * p + 1, part])


def unpack_heads(x):
    heads, rows, _ = x.shape
    rows //= 2
    width = WIDE * PAIR
    part = pl.BlockSpec((rows, width), lambda i: (0, i))
    return pl.pallas_call(
        unpack_kernel,
        out_shape=(jax.ShapeDtypeStruct((rows, heads * HEAD_DIM), x.dtype),) * 4,
        grid=(heads * HEAD_DIM // width,),
        in_specs=[pl.BlockSpec((2 * WIDE, 2 * rows, PAIR), lambda i: (i, 0, 0))],
        out_specs=(part,) * 4,
        compiler_params=pltpu.CompilerParams(vmem_limit_bytes=60 << 20),
        name="unpack_heads",
    )(x)


def attention_kernel(
    pattern_ref, valid_ref, start_ref, x_hbm, before_ref, after_ref,
    z_hbm, first_ref, last_ref, down_ref, up_ref,
    kv_ref, qg_ref, acc_ref, od_ref, dkv_ref, both_ref, pd_ref, in_sems, od_sems, dkv_sems,
    *, keys_num, group, lines,
):
    shards, rows = od_ref.shape[:2]
    edge = before_ref.shape[0]
    each = rows // BLOCK

    def fetch(source, i):
        return pltpu.make_async_copy(source, kv_ref.at[pl.ds(i * rows, rows)], in_sems.at[i])

    copies = [fetch(x_hbm.at[t, pl.ds(0, rows)], edge + t) for t in range(shards)]
    copies += [fetch(before_ref.at[t], t) for t in range(edge)]
    copies += [fetch(after_ref.at[t], edge + shards + t) for t in range(edge)]
    copies += [
        pltpu.make_async_copy(x_hbm.at[:, pl.ds(rows, rows)], qg_ref, in_sems.at[len(copies)])
    ]
    for copy in copies:
        copy.start()
    acc_ref[...] = jnp.zeros_like(acc_ref)
    for copy in copies:
        copy.wait()

    start = start_ref[0]
    low = lax.broadcasted_iota(jnp.int32, (BLOCK, PAIR), 1) < HEAD_DIM
    lane = lax.broadcasted_iota(jnp.int32, (1, PAIR), 1)

    def send_od(t):
        return pltpu.make_async_copy(od_ref.at[t], z_hbm.at[t, pl.ds(rows, rows)], od_sems.at[t])

    def send_dkv(t):
        return pltpu.make_async_copy(dkv_ref.at[t], z_hbm.at[t, pl.ds(0, rows)], dkv_sems.at[t])

    def one_group(t, _):
        meta = []
        for u in range(group):
            base = (t * group + u) * keys_num
            slots = [pattern_ref[base + j] for j in range(keys_num)]
            counts = [valid_ref[start + slot] for slot in slots]
            meta.append((u // each, slice(u % each * BLOCK, (u % each + 1) * BLOCK), slots, counts))
        shard = t * (group // each)

        def gathered(slots):
            return jnp.concatenate(
                [kv_ref[pl.ds(pl.multiple_of(slot * BLOCK, BLOCK), BLOCK), :] for slot in slots],
                axis=0,
            )

        def spread(s, part):
            qg = qg_ref[shard + s, part, :]
            zero = jnp.zeros_like(qg)
            return jnp.concatenate([jnp.where(low, zero, qg), jnp.where(low, qg, zero)], axis=0)

        for u, (s, part, slots, counts) in enumerate(meta):
            both_ref[u] = lax.dot_general(
                spread(s, part), gathered(slots), (((1,), (1,)), ((), ())),
                preferred_element_type=jnp.float32,
            )
        for u, (s, part, slots, counts) in enumerate(meta):
            bias = jnp.concatenate(
                [
                    jnp.where(
                        lane < jnp.where(lane < HEAD_DIM, counts[j], counts[j + 1] + HEAD_DIM),
                        0.0,
                        -jnp.inf,
                    )
                    for j in range(0, keys_num, 2)
                ],
                axis=1,
            )
            for r in range(0, BLOCK, lines):
                scores = both_ref[u, BLOCK + r : BLOCK + r + lines, :] + bias
                top = jnp.max(scores, axis=1, keepdims=True)
                weight = jnp.exp2((scores - top) * exp2_scale)
                total = jnp.sum(weight, axis=1, keepdims=True)
                prob = (weight * (1.0 / total)).astype(jnp.bfloat16)
                prob_wide = prob.astype(jnp.float32)
                grad_prob = both_ref[u, r : r + lines, :]
                delta = jnp.sum(prob_wide * grad_prob, axis=1, keepdims=True)
                dscore = (prob_wide * (grad_prob - delta)).astype(jnp.bfloat16)
                pd_ref[u, r : r + lines, :] = prob
                pd_ref[u, BLOCK + r : BLOCK + r + lines, :] = dscore
        for u, (s, part, slots, counts) in enumerate(meta):
            od = jnp.dot(pd_ref[u], gathered(slots), preferred_element_type=jnp.float32)
            od_ref[shard + s, part, :] = jnp.where(
                low, od[BLOCK:] * score_scale, od[:BLOCK]
            ).astype(od_ref.dtype)
        for s in range(group // each):
            send_od(shard + s).start()
        for u, (s, part, slots, counts) in enumerate(meta):
            dkv = lax.dot_general(
                pd_ref[u], spread(s, part), (((0,), (0,)), ((), ())),
                preferred_element_type=jnp.float32,
            )
            for j, slot in enumerate(slots):
                span = pl.ds(pl.multiple_of(slot * BLOCK, BLOCK), BLOCK)
                acc_ref[span, :] += dkv[j * BLOCK : (j + 1) * BLOCK]
        return 0

    lax.fori_loop(0, shards * each // group, one_group, 0)

    wide_low = lax.broadcasted_iota(jnp.int32, (rows, PAIR), 1) < HEAD_DIM

    def scaled(s):
        tile = acc_ref[s * rows : (s + 1) * rows, :]
        return jnp.where(wide_low, tile * score_scale, tile)

    for s in range(edge):
        down_ref[s] = scaled(s).astype(down_ref.dtype)
        up_ref[s] = scaled(edge + shards + s).astype(up_ref.dtype)
        first_ref[s] = scaled(edge + s)
        last_ref[s] = scaled(shards + s)
    for t in range(edge, shards - edge):
        dkv_ref[t] = scaled(edge + t).astype(dkv_ref.dtype)
        send_dkv(t).start()
    for t in range(shards):
        send_od(t).wait()
    for t in range(edge, shards - edge):
        send_dkv(t).wait()


def attention(pattern, valid_rows, start, x, before, after, group=16, lines=16):
    keys_num = pattern.shape[1]
    shards, rows = x.shape[0], x.shape[1] // 2
    edge = before.shape[0]
    ext = shards + 2 * edge
    smem = pl.BlockSpec(memory_space=pltpu.SMEM)
    hbm = pl.BlockSpec(memory_space=pltpu.HBM)
    vmem = pl.BlockSpec(memory_space=pltpu.VMEM)
    face = (edge, rows, PAIR)
    return pl.pallas_call(
        partial(attention_kernel, keys_num=keys_num, group=group, lines=lines),
        out_shape=(pltpu.HBM(x.shape, x.dtype),)
        + (pltpu.VMEM(face, jnp.float32),) * 2
        + (pltpu.VMEM(face, x.dtype),) * 2,
        in_specs=[smem, smem, smem, hbm, vmem, vmem],
        out_specs=(hbm, vmem, vmem, vmem, vmem),
        scratch_shapes=[
            pltpu.VMEM((ext * rows, PAIR), x.dtype),
            pltpu.VMEM((shards, rows, PAIR), x.dtype),
            pltpu.VMEM((ext * rows, PAIR), jnp.float32),
            pltpu.VMEM((shards, rows, PAIR), x.dtype),
            pltpu.VMEM((shards, rows, PAIR), x.dtype),
            pltpu.VMEM((group, PAIR, keys_num * BLOCK), jnp.float32),
            pltpu.VMEM((group, PAIR, keys_num * BLOCK), x.dtype),
            pltpu.SemaphoreType.DMA((ext + 1,)),
            pltpu.SemaphoreType.DMA((shards,)),
            pltpu.SemaphoreType.DMA((shards,)),
        ],
        compiler_params=pltpu.CompilerParams(vmem_limit_bytes=32 << 20),
        name="block_attention",
    )(pattern.reshape(-1), valid_rows, start, off_chip(x), on_chip(before), on_chip(after))


def join_kernel(z_in, first_ref, last_ref, low_ref, high_ref, z_hbm, sum_ref, sems):
    edge, rows = first_ref.shape[:2]
    shards = z_hbm.shape[0]
    sum_ref[0] = (first_ref[...] + low_ref[...].astype(jnp.float32)).astype(sum_ref.dtype)
    sum_ref[1] = (last_ref[...] + high_ref[...].astype(jnp.float32)).astype(sum_ref.dtype)
    copies = [
        pltpu.make_async_copy(
            sum_ref.at[i], z_hbm.at[pl.ds(at, edge), pl.ds(0, rows)], sems.at[i]
        )
        for i, at in enumerate((0, shards - edge))
    ]
    for copy in copies:
        copy.start()
    for copy in copies:
        copy.wait()


def join_faces(z, first, last, low, high):
    hbm = pl.BlockSpec(memory_space=pltpu.HBM)
    vmem = pl.BlockSpec(memory_space=pltpu.VMEM)
    return pl.pallas_call(
        join_kernel,
        out_shape=pltpu.HBM(z.shape, z.dtype),
        in_specs=[hbm, vmem, vmem, vmem, vmem],
        out_specs=hbm,
        scratch_shapes=[pltpu.VMEM((2, *low.shape), z.dtype), pltpu.SemaphoreType.DMA((2,))],
        input_output_aliases={0: 0},
        compiler_params=pltpu.CompilerParams(vmem_limit_bytes=8 << 20),
        name="join_faces",
    )(z, *(on_chip(a) for a in (first, last, low, high)))


def body(query, key, value, grad_out, pattern, valid_rows):
    def exchange(x):
        return lax.all_to_all(x, "seq", split_axis=0, concat_axis=0, tiled=True)

    size = lax.axis_size("slab")
    up = [(i, i + 1) for i in range(size - 1)]
    down = [(i + 1, i) for i in range(size - 1)]
    rows = query.shape[0]
    edge = FACE * BLOCK // rows
    x = exchange(pack_heads(key, value, query, grad_out))
    first, last = take_faces(x, edge, rows)
    before = lax.ppermute(last, "slab", up)
    after = lax.ppermute(first, "slab", down)
    start = (lax.axis_index("slab") * pattern.shape[0] - FACE).astype(jnp.int32).reshape(1)
    z, first, last, to_before, to_after = attention(pattern, valid_rows, start, x, before, after)
    high = lax.ppermute(to_before, "slab", down)
    low = lax.ppermute(to_after, "slab", up)
    z = exchange(join_faces(z, first, last, low, high))
    grad_key, grad_value, grad_query, attn_out = unpack_heads(z)
    return (attn_out, grad_query, grad_key, grad_value)


def solution(mesh):
    rows = P(("slab", "seq"), None)
    return jax.shard_map(
        body,
        mesh=mesh,
        in_specs=(rows, rows, rows, rows, P("slab", None), P()),
        out_specs=(rows, rows, rows, rows),
        check_vma=False,
    )
```

```python
from functools import partial
import math

import jax
import jax.numpy as jnp
from jax import lax
from jax.experimental import pallas as pl
from jax.experimental.pallas import tpu as pltpu
from jax.sharding import PartitionSpec as P

HEAD_DIM = 64
BLOCK = 64
FACE = 16
PAIR = 2 * HEAD_DIM
WIDE = 4

score_scale = 0.125
exp2_scale = score_scale * math.log2(math.e)


def on_chip(x):
    return pltpu.with_memory_space_constraint(x, pltpu.VMEM)


def off_chip(x):
    return pltpu.with_memory_space_constraint(x, pltpu.HBM)


def faces_kernel(x_hbm, first_ref, last_ref, sems):
    edge, rows = first_ref.shape[:2]
    copies = [
        pltpu.make_async_copy(x_hbm.at[pl.ds(at, edge), pl.ds(0, rows)], ref, sems.at[i])
        for i, (at, ref) in enumerate(((0, first_ref), (x_hbm.shape[0] - edge, last_ref)))
    ]
    for copy in copies:
        copy.start()
    for copy in copies:
        copy.wait()


def take_faces(x, edge, rows):
    vmem = pl.BlockSpec(memory_space=pltpu.VMEM)
    return pl.pallas_call(
        faces_kernel,
        out_shape=(pltpu.VMEM((edge, rows, PAIR), x.dtype),) * 2,
        in_specs=[pl.BlockSpec(memory_space=pltpu.HBM)],
        out_specs=(vmem, vmem),
        scratch_shapes=[pltpu.SemaphoreType.DMA((2,))],
        compiler_params=pltpu.CompilerParams(vmem_limit_bytes=4 << 20),
        name="take_faces",
    )(off_chip(x))


def swap_halves(a, b):
    low = jnp.concatenate([a[:, :HEAD_DIM], b[:, :HEAD_DIM]], axis=1)
    high = jnp.concatenate([a[:, HEAD_DIM:], b[:, HEAD_DIM:]], axis=1)
    return low, high


def pack_kernel(k_ref, v_ref, q_ref, g_ref, one_ref, two_ref):
    rows, half = k_ref.shape[0], two_ref.shape[1]
    for p in range(k_ref.shape[1] // PAIR):
        cols = slice(p * PAIR, (p + 1) * PAIR)
        for i, pair in enumerate(swap_halves(k_ref[:, cols], v_ref[:, cols])):
            one_ref[2 * p + i, :rows] = pair
        for i, pair in enumerate(swap_halves(q_ref[:, cols], g_ref[:, cols])):
            one_ref[2 * p + i, rows:] = pair[:half]
            two_ref[2 * p + i] = pair[half:]


def pack_heads(k, v, q, g):
    rows, cols = k.shape
    heads, half = cols // HEAD_DIM, rows // 2
    width = WIDE * PAIR
    part = pl.BlockSpec((rows, width), lambda i: (0, i))
    sizes = (rows + half, half)
    return pl.pallas_call(
        pack_kernel,
        out_shape=tuple(pltpu.HBM((heads, size, PAIR), k.dtype) for size in sizes),
        grid=(cols // width,),
        in_specs=[part] * 4,
        out_specs=tuple(pl.BlockSpec((2 * WIDE, size, PAIR), lambda i: (i, 0, 0)) for size in sizes),
        compiler_params=pltpu.CompilerParams(vmem_limit_bytes=60 << 20),
        name="pack_heads",
    )(k, v, q, g)


def unpack_kernel(one_ref, two_ref, k_ref, v_ref, q_ref, o_ref):
    rows, half = k_ref.shape[0], two_ref.shape[1]
    for p in range(k_ref.shape[1] // PAIR):
        cols = slice(p * PAIR, (p + 1) * PAIR)
        h, i = 2 * p, 2 * p + 1
        k_ref[:, cols], v_ref[:, cols] = swap_halves(one_ref[h, :rows], one_ref[i, :rows])
        q_ref[:half, cols], o_ref[:half, cols] = swap_halves(two_ref[h], two_ref[i])
        q_ref[half:, cols], o_ref[half:, cols] = swap_halves(one_ref[h, rows:], one_ref[i, rows:])


def unpack_heads(one, two):
    heads, half, _ = two.shape
    rows = 2 * half
    width = WIDE * PAIR
    part = pl.BlockSpec((rows, width), lambda i: (0, i))
    return pl.pallas_call(
        unpack_kernel,
        out_shape=(jax.ShapeDtypeStruct((rows, heads * HEAD_DIM), one.dtype),) * 4,
        grid=(heads * HEAD_DIM // width,),
        in_specs=[
            pl.BlockSpec((2 * WIDE, x.shape[1], PAIR), lambda i: (i, 0, 0)) for x in (one, two)
        ],
        out_specs=(part,) * 4,
        compiler_params=pltpu.CompilerParams(vmem_limit_bytes=60 << 20),
        name="unpack_heads",
    )(off_chip(one), off_chip(two))


def query_blocks(
    pattern_ref, valid_ref, start_ref, kv_ref, qg_ref, acc_ref, od_ref, both_ref, pd_ref, send_od,
    *, keys_num, chunk, group, lines, ready=None,
):
    shards, rows = qg_ref.shape[:2]
    each = rows // BLOCK
    start = start_ref[0]
    low = lax.broadcasted_iota(jnp.int32, (BLOCK, PAIR), 1) < HEAD_DIM
    lane = lax.broadcasted_iota(jnp.int32, (1, PAIR), 1)

    def one_group(t, _):
        shard = t * (group // each)
        meta = []
        for u in range(group):
            s, i = u // each, u % each
            base = ((shard + s) * 2 * each + chunk * each + i) * keys_num
            slots = [pattern_ref[base + j] for j in range(keys_num)]
            counts = [valid_ref[start + slot] for slot in slots]
            meta.append((s, slice(i * BLOCK, (i + 1) * BLOCK), slots, counts))

        def gathered(slots):
            return jnp.concatenate(
                [kv_ref[pl.ds(pl.multiple_of(slot * BLOCK, BLOCK), BLOCK), :] for slot in slots],
                axis=0,
            )

        def spread(s, part):
            qg = qg_ref[shard + s, part, :]
            zero = jnp.zeros_like(qg)
            return jnp.concatenate([jnp.where(low, zero, qg), jnp.where(low, qg, zero)], axis=0)

        for u, (s, part, slots, counts) in enumerate(meta):
            both_ref[u] = lax.dot_general(
                spread(s, part), gathered(slots), (((1,), (1,)), ((), ())),
                preferred_element_type=jnp.float32,
            )
        for u, (s, part, slots, counts) in enumerate(meta):
            bias = jnp.concatenate(
                [
                    jnp.where(
                        lane < jnp.where(lane < HEAD_DIM, counts[j], counts[j + 1] + HEAD_DIM),
                        0.0,
                        -jnp.inf,
                    )
                    for j in range(0, keys_num, 2)
                ],
                axis=1,
            )
            for r in range(0, BLOCK, lines):
                scores = both_ref[u, BLOCK + r : BLOCK + r + lines, :] + bias
                top = jnp.max(scores, axis=1, keepdims=True)
                weight = jnp.exp2((scores - top) * exp2_scale)
                total = jnp.sum(weight, axis=1, keepdims=True)
                prob = (weight * (1.0 / total)).astype(jnp.bfloat16)
                prob_wide = prob.astype(jnp.float32)
                grad_prob = both_ref[u, r : r + lines, :]
                delta = jnp.sum(prob_wide * grad_prob, axis=1, keepdims=True)
                dscore = (prob_wide * (grad_prob - delta)).astype(jnp.bfloat16)
                pd_ref[u, r : r + lines, :] = prob
                pd_ref[u, BLOCK + r : BLOCK + r + lines, :] = dscore
        for u, (s, part, slots, counts) in enumerate(meta):
            od = jnp.dot(pd_ref[u], gathered(slots), preferred_element_type=jnp.float32)
            od_ref[shard + s, part, :] = jnp.where(
                low, od[BLOCK:] * score_scale, od[:BLOCK]
            ).astype(od_ref.dtype)
        for s in range(group // each):
            send_od(shard + s).start()
        if ready is not None:
            pl.when(t == 0)(ready)
        for u, (s, part, slots, counts) in enumerate(meta):
            dkv = lax.dot_general(
                pd_ref[u], spread(s, part), (((0,), (0,)), ((), ())),
                preferred_element_type=jnp.float32,
            )
            for j, slot in enumerate(slots):
                span = pl.ds(pl.multiple_of(slot * BLOCK, BLOCK), BLOCK)
                acc_ref[span, :] += dkv[j * BLOCK : (j + 1) * BLOCK]
        return 0

    lax.fori_loop(0, shards * each // group, one_group, 0)


def first_kernel(
    pattern_ref, valid_ref, start_ref, x_hbm, before_ref, after_ref,
    od_hbm, kv_hbm, acc_hbm,
    kv_ref, acc_ref, qg_ref, od_ref, both_ref, pd_ref, in_sems, od_sems, out_sems, **sizes,
):
    shards, half = qg_ref.shape[:2]
    rows = x_hbm.shape[1] - half
    edge = before_ref.shape[0]

    def fetch(source, i):
        return pltpu.make_async_copy(source, kv_ref.at[pl.ds(i * rows, rows)], in_sems.at[i])

    copies = [fetch(x_hbm.at[t, pl.ds(0, rows)], edge + t) for t in range(shards)]
    copies += [fetch(before_ref.at[t], t) for t in range(edge)]
    copies += [fetch(after_ref.at[t], edge + shards + t) for t in range(edge)]
    copies += [
        pltpu.make_async_copy(x_hbm.at[:, pl.ds(rows, half)], qg_ref, in_sems.at[len(copies)])
    ]
    for copy in copies:
        copy.start()
    acc_ref[...] = jnp.zeros_like(acc_ref)
    for copy in copies:
        copy.wait()
    keep = pltpu.make_async_copy(kv_ref, kv_hbm, out_sems.at[0])
    keep.start()

    def send_od(t):
        return pltpu.make_async_copy(od_ref.at[t], od_hbm.at[t], od_sems.at[t])

    query_blocks(
        pattern_ref, valid_ref, start_ref, kv_ref, qg_ref, acc_ref, od_ref, both_ref, pd_ref,
        send_od, chunk=0, **sizes,
    )
    total = pltpu.make_async_copy(acc_ref, acc_hbm, out_sems.at[1])
    total.start()
    for t in range(shards):
        send_od(t).wait()
    keep.wait()
    total.wait()


def second_kernel(
    pattern_ref, valid_ref, start_ref, x_hbm, kv_hbm, acc_hbm,
    z_hbm, first_ref, last_ref, down_ref, up_ref,
    kv_ref, acc_ref, qg_ref, od_ref, dkv_ref, both_ref, pd_ref, in_sems, od_sems, dkv_sems, **sizes,
):
    shards, half = qg_ref.shape[:2]
    rows = 2 * half
    edge = first_ref.shape[0]
    copies = [
        pltpu.make_async_copy(source, target, in_sems.at[i])
        for i, (source, target) in enumerate(((x_hbm, qg_ref), (kv_hbm, kv_ref), (acc_hbm, acc_ref)))
    ]
    for copy in copies:
        copy.start()
    copies[0].wait()
    copies[1].wait()

    def send_od(t):
        return pltpu.make_async_copy(od_ref.at[t], z_hbm.at[t, pl.ds(rows, half)], od_sems.at[t])

    def send_dkv(t):
        return pltpu.make_async_copy(dkv_ref.at[t], z_hbm.at[t, pl.ds(0, rows)], dkv_sems.at[t])

    query_blocks(
        pattern_ref, valid_ref, start_ref, kv_ref, qg_ref, acc_ref, od_ref, both_ref, pd_ref,
        send_od, chunk=1, ready=copies[2].wait, **sizes,
    )
    low = lax.broadcasted_iota(jnp.int32, (rows, PAIR), 1) < HEAD_DIM

    def scaled(s):
        tile = acc_ref[s * rows : (s + 1) * rows, :]
        return jnp.where(low, tile * score_scale, tile)

    for t in range(edge, shards - edge):
        dkv_ref[t] = scaled(edge + t).astype(dkv_ref.dtype)
        send_dkv(t).start()
    for s in range(edge):
        down_ref[s] = scaled(s).astype(down_ref.dtype)
        up_ref[s] = scaled(edge + shards + s).astype(up_ref.dtype)
        first_ref[s] = scaled(edge + s)
        last_ref[s] = scaled(shards + s)
    for t in range(shards):
        send_od(t).wait()
    for t in range(edge, shards - edge):
        send_dkv(t).wait()


def cost(tokens, keys_num):
    work = tokens * keys_num * BLOCK
    return pl.CostEstimate(flops=12 * PAIR * work, transcendentals=work, bytes_accessed=16 << 20)


def first_half(pattern, valid_rows, start, x, before, after, group=16, lines=16):
    keys_num = pattern.shape[0] * BLOCK // (x.shape[0] * before.shape[1])
    shards, edge, rows = x.shape[0], before.shape[0], before.shape[1]
    half, ext = rows // 2, shards + 2 * edge
    smem = pl.BlockSpec(memory_space=pltpu.SMEM)
    hbm = pl.BlockSpec(memory_space=pltpu.HBM)
    vmem = pl.BlockSpec(memory_space=pltpu.VMEM)
    return pl.pallas_call(
        partial(first_kernel, keys_num=keys_num, group=group, lines=lines),
        out_shape=(
            pltpu.HBM((shards, half, PAIR), x.dtype),
            pltpu.HBM((ext * rows, PAIR), x.dtype),
            pltpu.HBM((ext * rows, PAIR), jnp.float32),
        ),
        in_specs=[smem, smem, smem, hbm, vmem, vmem],
        out_specs=(hbm, hbm, hbm),
        scratch_shapes=[
            pltpu.VMEM((ext * rows, PAIR), x.dtype),
            pltpu.VMEM((ext * rows, PAIR), jnp.float32),
            pltpu.VMEM((shards, half, PAIR), x.dtype),
            pltpu.VMEM((shards, half, PAIR), x.dtype),
            pltpu.VMEM((group, PAIR, keys_num * BLOCK), jnp.float32),
            pltpu.VMEM((group, PAIR, keys_num * BLOCK), x.dtype),
            pltpu.SemaphoreType.DMA((ext + 1,)),
            pltpu.SemaphoreType.DMA((shards,)),
            pltpu.SemaphoreType.DMA((2,)),
        ],
        compiler_params=pltpu.CompilerParams(vmem_limit_bytes=32 << 20),
        cost_estimate=cost(shards * half, keys_num),
        name="first_half",
    )(pattern, valid_rows, start, off_chip(x), on_chip(before), on_chip(after))


def second_half(pattern, valid_rows, start, x, kv, acc, edge, group=16, lines=16):
    shards, half = x.shape[:2]
    rows = 2 * half
    keys_num = pattern.shape[0] * BLOCK // (shards * rows)
    smem = pl.BlockSpec(memory_space=pltpu.SMEM)
    hbm = pl.BlockSpec(memory_space=pltpu.HBM)
    vmem = pl.BlockSpec(memory_space=pltpu.VMEM)
    face = (edge, rows, PAIR)
    return pl.pallas_call(
        partial(second_kernel, keys_num=keys_num, group=group, lines=lines),
        out_shape=(pltpu.HBM((shards, rows + half, PAIR), x.dtype),)
        + (pltpu.VMEM(face, jnp.float32),) * 2
        + (pltpu.VMEM(face, x.dtype),) * 2,
        in_specs=[smem, smem, smem, hbm, hbm, hbm],
        out_specs=(hbm, vmem, vmem, vmem, vmem),
        scratch_shapes=[
            pltpu.VMEM(kv.shape, kv.dtype),
            pltpu.VMEM(acc.shape, acc.dtype),
            pltpu.VMEM((shards, half, PAIR), x.dtype),
            pltpu.VMEM((shards, half, PAIR), x.dtype),
            pltpu.VMEM((shards, rows, PAIR), x.dtype),
            pltpu.VMEM((group, PAIR, keys_num * BLOCK), jnp.float32),
            pltpu.VMEM((group, PAIR, keys_num * BLOCK), x.dtype),
            pltpu.SemaphoreType.DMA((3,)),
            pltpu.SemaphoreType.DMA((shards,)),
            pltpu.SemaphoreType.DMA((shards,)),
        ],
        compiler_params=pltpu.CompilerParams(vmem_limit_bytes=32 << 20),
        cost_estimate=cost(shards * half, keys_num),
        name="second_half",
    )(pattern, valid_rows, start, off_chip(x), off_chip(kv), off_chip(acc))


def join_kernel(z_in, first_ref, last_ref, low_ref, high_ref, z_hbm, sum_ref, sems):
    edge, rows = first_ref.shape[:2]
    shards = z_hbm.shape[0]
    sum_ref[0] = (first_ref[...] + low_ref[...].astype(jnp.float32)).astype(sum_ref.dtype)
    sum_ref[1] = (last_ref[...] + high_ref[...].astype(jnp.float32)).astype(sum_ref.dtype)
    copies = [
        pltpu.make_async_copy(
            sum_ref.at[i], z_hbm.at[pl.ds(at, edge), pl.ds(0, rows)], sems.at[i]
        )
        for i, at in enumerate((0, shards - edge))
    ]
    for copy in copies:
        copy.start()
    for copy in copies:
        copy.wait()


def join_faces(z, first, last, low, high):
    hbm = pl.BlockSpec(memory_space=pltpu.HBM)
    vmem = pl.BlockSpec(memory_space=pltpu.VMEM)
    return pl.pallas_call(
        join_kernel,
        out_shape=pltpu.HBM(z.shape, z.dtype),
        in_specs=[hbm, vmem, vmem, vmem, vmem],
        out_specs=hbm,
        scratch_shapes=[pltpu.VMEM((2, *low.shape), z.dtype), pltpu.SemaphoreType.DMA((2,))],
        input_output_aliases={0: 0},
        compiler_params=pltpu.CompilerParams(vmem_limit_bytes=8 << 20),
        name="join_faces",
    )(z, *(on_chip(a) for a in (first, last, low, high)))


def body(query, key, value, grad_out, pattern, valid_rows):
    def exchange(x):
        return lax.all_to_all(x, "seq", split_axis=0, concat_axis=0, tiled=True)

    size = lax.axis_size("slab")
    up = [(i, i + 1) for i in range(size - 1)]
    down = [(i + 1, i) for i in range(size - 1)]
    rows = query.shape[0]
    edge = FACE * BLOCK // rows
    one, two = pack_heads(key, value, query, grad_out)
    one = exchange(one)
    first, last = take_faces(one, edge, rows)
    before = lax.ppermute(last, "slab", up)
    after = lax.ppermute(first, "slab", down)
    two = exchange(two)
    start = (lax.axis_index("slab") * pattern.shape[0] - FACE).astype(jnp.int32).reshape(1)
    scalars = (pattern.reshape(-1), valid_rows, start)
    od, kv, acc = first_half(*scalars, one, before, after)
    od = exchange(od)
    z, first, last, to_before, to_after = second_half(*scalars, two, kv, acc, edge)
    high = lax.ppermute(to_before, "slab", down)
    low = lax.ppermute(to_after, "slab", up)
    z = exchange(join_faces(z, first, last, low, high))
    grad_key, grad_value, grad_query, attn_out = unpack_heads(z, od)
    return (attn_out, grad_query, grad_key, grad_value)


def solution(mesh):
    rows = P(("slab", "seq"), None)
    return jax.shard_map(
        body,
        mesh=mesh,
        in_specs=(rows, rows, rows, rows, P("slab", None), P()),
        out_specs=(rows, rows, rows, rows),
        check_vma=False,
    )
```

```python
from functools import partial
import math

import jax
import jax.numpy as jnp
from jax import lax
from jax.experimental import pallas as pl
from jax.experimental.pallas import tpu as pltpu
from jax.sharding import PartitionSpec as P

HEAD_DIM = 64
BLOCK = 64
FACE = 16
PAIR = 2 * HEAD_DIM
CHUNKS = 4

score_scale = 0.125
exp2_scale = score_scale * math.log2(math.e)


def on_chip(x):
    return pltpu.with_memory_space_constraint(x, pltpu.VMEM)


def off_chip(x):
    return pltpu.with_memory_space_constraint(x, pltpu.HBM)


def faces_kernel(x_hbm, first_ref, last_ref, sems):
    edge, rows = first_ref.shape[:2]
    copies = [
        pltpu.make_async_copy(x_hbm.at[pl.ds(at, edge), pl.ds(0, rows)], ref, sems.at[i])
        for i, (at, ref) in enumerate(((0, first_ref), (x_hbm.shape[0] - edge, last_ref)))
    ]
    for copy in copies:
        copy.start()
    for copy in copies:
        copy.wait()


def take_faces(x, edge, rows):
    vmem = pl.BlockSpec(memory_space=pltpu.VMEM)
    return pl.pallas_call(
        faces_kernel,
        out_shape=(pltpu.VMEM((edge, rows, PAIR), x.dtype),) * 2,
        in_specs=[pl.BlockSpec(memory_space=pltpu.HBM)],
        out_specs=(vmem, vmem),
        scratch_shapes=[pltpu.SemaphoreType.DMA((2,))],
        compiler_params=pltpu.CompilerParams(vmem_limit_bytes=4 << 20),
        name="take_faces",
    )(off_chip(x))


def swap_halves(a, b):
    low = jnp.concatenate([a[:, :HEAD_DIM], b[:, :HEAD_DIM]], axis=1)
    high = jnp.concatenate([a[:, HEAD_DIM:], b[:, HEAD_DIM:]], axis=1)
    return low, high


def pack_kernel(
    k_hbm, v_hbm, q_hbm, g_hbm, one_hbm, two_hbm, in_refs, out_refs, in_sems, one_sems, two_sems,
):
    rows, half = k_hbm.shape[0], two_hbm.shape[1]
    chunk = rows // CHUNKS
    pairs = ((k_hbm, v_hbm), (q_hbm, g_hbm))

    def span(c):
        return pl.ds(c * chunk, chunk)

    def load(n, i, c):
        return pltpu.make_async_copy(
            pairs[n][i].at[span(c)], in_refs.at[2 * n + i, span(c)], in_sems.at[2 * n + i, c]
        )

    def store(n, c):
        if n == 0 or c * chunk < half:
            target = one_hbm.at[:, pl.ds(n * rows + c * chunk, chunk)]
        else:
            target = two_hbm.at[:, pl.ds(c * chunk - half, chunk)]
        return pltpu.make_async_copy(
            out_refs.at[n, :, span(c)], target, (one_sems if n == 0 else two_sems).at[c]
        )

    order = [(n, c) for n in range(2) for c in range(CHUNKS)]
    for n, c in order:
        for i in range(2):
            load(n, i, c).start()
    for n, c in order:
        for i in range(2):
            load(n, i, c).wait()
        part = slice(c * chunk, (c + 1) * chunk)
        for p in range(k_hbm.shape[1] // PAIR):
            cols = slice(p * PAIR, (p + 1) * PAIR)
            halves = swap_halves(in_refs[2 * n, part, cols], in_refs[2 * n + 1, part, cols])
            out_refs[n, 2 * p, part], out_refs[n, 2 * p + 1, part] = halves
        store(n, c).start()
    for n, c in order:
        store(n, c).wait()


def pack_heads(k, v, q, g):
    rows, cols = k.shape
    heads, half = cols // HEAD_DIM, rows // 2
    hbm = pl.BlockSpec(memory_space=pltpu.HBM)
    return pl.pallas_call(
        pack_kernel,
        out_shape=tuple(pltpu.HBM((heads, size, PAIR), k.dtype) for size in (rows + half, half)),
        in_specs=[hbm] * 4,
        out_specs=(hbm, hbm),
        scratch_shapes=[
            pltpu.VMEM((4, rows, cols), k.dtype),
            pltpu.VMEM((2, heads, rows, PAIR), k.dtype),
            pltpu.SemaphoreType.DMA((4, CHUNKS)),
            pltpu.SemaphoreType.DMA((CHUNKS,)),
            pltpu.SemaphoreType.DMA((CHUNKS,)),
        ],
        compiler_params=pltpu.CompilerParams(vmem_limit_bytes=60 << 20),
        name="pack_heads",
    )(*(off_chip(x) for x in (k, v, q, g)))


def unpack_kernel(
    one_hbm, two_hbm, k_hbm, v_hbm, q_hbm, o_hbm, in_refs, out_refs, one_sems, two_sems, out_sems,
):
    rows, half = k_hbm.shape[0], two_hbm.shape[1]
    chunk = rows // CHUNKS
    pairs = ((k_hbm, v_hbm), (q_hbm, o_hbm))

    def span(c):
        return pl.ds(c * chunk, chunk)

    def load(n, c):
        if n == 0:
            source = one_hbm.at[:, span(c)]
        elif c * chunk < half:
            source = two_hbm.at[:, span(c)]
        else:
            source = one_hbm.at[:, pl.ds(rows + c * chunk - half, chunk)]
        return pltpu.make_async_copy(
            source, in_refs.at[n, :, span(c)], (one_sems if n == 0 else two_sems).at[c]
        )

    def store(n, i, c):
        return pltpu.make_async_copy(
            out_refs.at[2 * n + i, span(c)], pairs[n][i].at[span(c)], out_sems.at[2 * n + i, c]
        )

    order = [(n, c) for n in range(2) for c in range(CHUNKS)]
    for n, c in order:
        load(n, c).start()
    for n, c in order:
        load(n, c).wait()
        part = slice(c * chunk, (c + 1) * chunk)
        for p in range(k_hbm.shape[1] // PAIR):
            cols = slice(p * PAIR, (p + 1) * PAIR)
            halves = swap_halves(in_refs[n, 2 * p, part], in_refs[n, 2 * p + 1, part])
            out_refs[2 * n, part, cols], out_refs[2 * n + 1, part, cols] = halves
        for i in range(2):
            store(n, i, c).start()
    for n, c in order:
        for i in range(2):
            store(n, i, c).wait()


def unpack_heads(one, two):
    heads, half, _ = two.shape
    rows, cols = 2 * half, heads * HEAD_DIM
    hbm = pl.BlockSpec(memory_space=pltpu.HBM)
    return pl.pallas_call(
        unpack_kernel,
        out_shape=(pltpu.HBM((rows, cols), one.dtype),) * 4,
        in_specs=[hbm, hbm],
        out_specs=(hbm,) * 4,
        scratch_shapes=[
            pltpu.VMEM((2, heads, rows, PAIR), one.dtype),
            pltpu.VMEM((4, rows, cols), one.dtype),
            pltpu.SemaphoreType.DMA((CHUNKS,)),
            pltpu.SemaphoreType.DMA((CHUNKS,)),
            pltpu.SemaphoreType.DMA((4, CHUNKS)),
        ],
        compiler_params=pltpu.CompilerParams(vmem_limit_bytes=60 << 20),
        name="unpack_heads",
    )(off_chip(one), off_chip(two))


def in_turn(*tasks):
    def steps(stage, blocks):
        for u in blocks:
            yield from stage(u)

    running = [steps(*task) for task in tasks]
    while running:
        running = [task for task in running if next(task, True) is None]


def query_blocks(
    pattern_ref, valid_ref, start_ref, kv_ref, qg_ref, acc_ref, od_ref, both_ref, pd_ref, send_od,
    *, keys_num, chunk, group, lines, ready=None,
):
    shards, rows = qg_ref.shape[:2]
    each = rows // BLOCK
    start = start_ref[0]
    low = lax.broadcasted_iota(jnp.int32, (BLOCK, PAIR), 1) < HEAD_DIM
    lane = lax.broadcasted_iota(jnp.int32, (1, PAIR), 1)

    def one_group(t, _):
        shard = t * (group // each)
        meta = []
        for u in range(group):
            s, i = u // each, u % each
            base = ((shard + s) * 2 * each + chunk * each + i) * keys_num
            slots = [pattern_ref[base + j] for j in range(keys_num)]
            counts = [valid_ref[start + slot] for slot in slots]
            meta.append((s, slice(i * BLOCK, (i + 1) * BLOCK), slots, counts))

        def gathered(slots):
            return jnp.concatenate(
                [kv_ref[pl.ds(pl.multiple_of(slot * BLOCK, BLOCK), BLOCK), :] for slot in slots],
                axis=0,
            )

        def spread(s, part):
            qg = qg_ref[shard + s, part, :]
            zero = jnp.zeros_like(qg)
            return jnp.concatenate([jnp.where(low, zero, qg), jnp.where(low, qg, zero)], axis=0)

        def probe(u):
            s, part, slots, counts = meta[u]
            kv, gq = gathered(slots), spread(s, part)
            for n in range(0, keys_num * BLOCK, 2 * PAIR):
                both_ref[u, :, n : n + 2 * PAIR] = lax.dot_general(
                    gq, kv[n : n + 2 * PAIR], (((1,), (1,)), ((), ())),
                    preferred_element_type=jnp.float32,
                )
                yield

        def weigh(u):
            s, part, slots, counts = meta[u]
            bias = jnp.concatenate(
                [
                    jnp.where(
                        lane < jnp.where(lane < HEAD_DIM, counts[j], counts[j + 1] + HEAD_DIM),
                        0.0,
                        -jnp.inf,
                    )
                    for j in range(0, keys_num, 2)
                ],
                axis=1,
            )
            for r in range(0, BLOCK, lines):
                scores = both_ref[u, BLOCK + r : BLOCK + r + lines, :] + bias
                top = jnp.max(scores, axis=1, keepdims=True)
                weight = jnp.exp2((scores - top) * exp2_scale)
                total = jnp.sum(weight, axis=1, keepdims=True)
                prob = (weight * (1.0 / total)).astype(jnp.bfloat16)
                prob_wide = prob.astype(jnp.float32)
                grad_prob = both_ref[u, r : r + lines, :]
                delta = jnp.sum(prob_wide * grad_prob, axis=1, keepdims=True)
                dscore = (prob_wide * (grad_prob - delta)).astype(jnp.bfloat16)
                pd_ref[u, r : r + lines, :] = prob
                pd_ref[u, BLOCK + r : BLOCK + r + lines, :] = dscore
                yield

        def rows_out(u):
            s, part, slots, counts = meta[u]
            od = jnp.dot(pd_ref[u], gathered(slots), preferred_element_type=jnp.float32)
            od_ref[shard + s, part, :] = jnp.where(
                low, od[BLOCK:] * score_scale, od[:BLOCK]
            ).astype(od_ref.dtype)
            yield

        def keys_out(u):
            s, part, slots, counts = meta[u]
            dkv = lax.dot_general(
                pd_ref[u], spread(s, part), (((0,), (0,)), ((), ())),
                preferred_element_type=jnp.float32,
            )
            yield
            for j, slot in enumerate(slots):
                span = pl.ds(pl.multiple_of(slot * BLOCK, BLOCK), BLOCK)
                acc_ref[span, :] += dkv[j * BLOCK : (j + 1) * BLOCK]
                if j % 2:
                    yield

        near, far = range(group // 2), range(group // 2, group)
        in_turn((probe, near))
        in_turn((probe, far), (weigh, near))
        if ready is not None:
            pl.when(t == 0)(ready)
        in_turn((keys_out, near), (weigh, far))
        in_turn((rows_out, range(group)))
        for s in range(group // each):
            send_od(shard + s).start()
        in_turn((keys_out, far))
        return 0

    lax.fori_loop(0, shards * each // group, one_group, 0)


def first_kernel(
    pattern_ref, valid_ref, start_ref, x_hbm, before_ref, after_ref,
    od_hbm, kv_hbm, acc_hbm,
    kv_ref, acc_ref, qg_ref, od_ref, both_ref, pd_ref, in_sems, od_sems, out_sems, **sizes,
):
    shards, half = qg_ref.shape[:2]
    rows = x_hbm.shape[1] - half
    edge = before_ref.shape[0]

    def fetch(source, i):
        return pltpu.make_async_copy(source, kv_ref.at[pl.ds(i * rows, rows)], in_sems.at[i])

    copies = [fetch(x_hbm.at[t, pl.ds(0, rows)], edge + t) for t in range(shards)]
    copies += [fetch(before_ref.at[t], t) for t in range(edge)]
    copies += [fetch(after_ref.at[t], edge + shards + t) for t in range(edge)]
    copies += [
        pltpu.make_async_copy(x_hbm.at[:, pl.ds(rows, half)], qg_ref, in_sems.at[len(copies)])
    ]
    for copy in copies:
        copy.start()
    acc_ref[...] = jnp.zeros_like(acc_ref)
    for copy in copies:
        copy.wait()
    keep = pltpu.make_async_copy(kv_ref, kv_hbm, out_sems.at[0])
    keep.start()

    def send_od(t):
        return pltpu.make_async_copy(od_ref.at[t], od_hbm.at[t], od_sems.at[t])

    query_blocks(
        pattern_ref, valid_ref, start_ref, kv_ref, qg_ref, acc_ref, od_ref, both_ref, pd_ref,
        send_od, chunk=0, **sizes,
    )
    total = pltpu.make_async_copy(acc_ref, acc_hbm, out_sems.at[1])
    total.start()
    for t in range(shards):
        send_od(t).wait()
    keep.wait()
    total.wait()


def second_kernel(
    pattern_ref, valid_ref, start_ref, x_hbm, kv_hbm, acc_hbm,
    z_hbm, first_ref, last_ref, down_ref, up_ref,
    kv_ref, acc_ref, qg_ref, od_ref, dkv_ref, both_ref, pd_ref, in_sems, od_sems, dkv_sems, **sizes,
):
    shards, half = qg_ref.shape[:2]
    rows = 2 * half
    edge = first_ref.shape[0]
    copies = [
        pltpu.make_async_copy(source, target, in_sems.at[i])
        for i, (source, target) in enumerate(((x_hbm, qg_ref), (kv_hbm, kv_ref), (acc_hbm, acc_ref)))
    ]
    for copy in copies:
        copy.start()
    copies[0].wait()
    copies[1].wait()

    def send_od(t):
        return pltpu.make_async_copy(od_ref.at[t], z_hbm.at[t, pl.ds(rows, half)], od_sems.at[t])

    def send_dkv(t):
        return pltpu.make_async_copy(dkv_ref.at[t], z_hbm.at[t, pl.ds(0, rows)], dkv_sems.at[t])

    query_blocks(
        pattern_ref, valid_ref, start_ref, kv_ref, qg_ref, acc_ref, od_ref, both_ref, pd_ref,
        send_od, chunk=1, ready=copies[2].wait, **sizes,
    )
    low = lax.broadcasted_iota(jnp.int32, (rows, PAIR), 1) < HEAD_DIM

    def scaled(s):
        tile = acc_ref[s * rows : (s + 1) * rows, :]
        return jnp.where(low, tile * score_scale, tile)

    for t in range(edge, shards - edge):
        dkv_ref[t] = scaled(edge + t).astype(dkv_ref.dtype)
        send_dkv(t).start()
    for s in range(edge):
        down_ref[s] = scaled(s).astype(down_ref.dtype)
        up_ref[s] = scaled(edge + shards + s).astype(up_ref.dtype)
        first_ref[s] = scaled(edge + s)
        last_ref[s] = scaled(shards + s)
    for t in range(shards):
        send_od(t).wait()
    for t in range(edge, shards - edge):
        send_dkv(t).wait()


def cost(tokens, keys_num):
    work = tokens * keys_num * BLOCK
    return pl.CostEstimate(flops=12 * PAIR * work, transcendentals=work, bytes_accessed=16 << 20)


def first_half(pattern, valid_rows, start, x, before, after, group=16, lines=16):
    keys_num = pattern.shape[0] * BLOCK // (x.shape[0] * before.shape[1])
    shards, edge, rows = x.shape[0], before.shape[0], before.shape[1]
    half, ext = rows // 2, shards + 2 * edge
    smem = pl.BlockSpec(memory_space=pltpu.SMEM)
    hbm = pl.BlockSpec(memory_space=pltpu.HBM)
    vmem = pl.BlockSpec(memory_space=pltpu.VMEM)
    return pl.pallas_call(
        partial(first_kernel, keys_num=keys_num, group=group, lines=lines),
        out_shape=(
            pltpu.HBM((shards, half, PAIR), x.dtype),
            pltpu.HBM((ext * rows, PAIR), x.dtype),
            pltpu.HBM((ext * rows, PAIR), jnp.float32),
        ),
        in_specs=[smem, smem, smem, hbm, vmem, vmem],
        out_specs=(hbm, hbm, hbm),
        scratch_shapes=[
            pltpu.VMEM((ext * rows, PAIR), x.dtype),
            pltpu.VMEM((ext * rows, PAIR), jnp.float32),
            pltpu.VMEM((shards, half, PAIR), x.dtype),
            pltpu.VMEM((shards, half, PAIR), x.dtype),
            pltpu.VMEM((group, PAIR, keys_num * BLOCK), jnp.float32),
            pltpu.VMEM((group, PAIR, keys_num * BLOCK), x.dtype),
            pltpu.SemaphoreType.DMA((ext + 1,)),
            pltpu.SemaphoreType.DMA((shards,)),
            pltpu.SemaphoreType.DMA((2,)),
        ],
        compiler_params=pltpu.CompilerParams(vmem_limit_bytes=32 << 20),
        cost_estimate=cost(shards * half, keys_num),
        name="first_half",
    )(pattern, valid_rows, start, off_chip(x), on_chip(before), on_chip(after))


def second_half(pattern, valid_rows, start, x, kv, acc, edge, group=16, lines=16):
    shards, half = x.shape[:2]
    rows = 2 * half
    keys_num = pattern.shape[0] * BLOCK // (shards * rows)
    smem = pl.BlockSpec(memory_space=pltpu.SMEM)
    hbm = pl.BlockSpec(memory_space=pltpu.HBM)
    vmem = pl.BlockSpec(memory_space=pltpu.VMEM)
    face = (edge, rows, PAIR)
    return pl.pallas_call(
        partial(second_kernel, keys_num=keys_num, group=group, lines=lines),
        out_shape=(pltpu.HBM((shards, rows + half, PAIR), x.dtype),)
        + (pltpu.VMEM(face, jnp.float32),) * 2
        + (pltpu.VMEM(face, x.dtype),) * 2,
        in_specs=[smem, smem, smem, hbm, hbm, hbm],
        out_specs=(hbm, vmem, vmem, vmem, vmem),
        scratch_shapes=[
            pltpu.VMEM(kv.shape, kv.dtype),
            pltpu.VMEM(acc.shape, acc.dtype),
            pltpu.VMEM((shards, half, PAIR), x.dtype),
            pltpu.VMEM((shards, half, PAIR), x.dtype),
            pltpu.VMEM((shards, rows, PAIR), x.dtype),
            pltpu.VMEM((group, PAIR, keys_num * BLOCK), jnp.float32),
            pltpu.VMEM((group, PAIR, keys_num * BLOCK), x.dtype),
            pltpu.SemaphoreType.DMA((3,)),
            pltpu.SemaphoreType.DMA((shards,)),
            pltpu.SemaphoreType.DMA((shards,)),
        ],
        compiler_params=pltpu.CompilerParams(vmem_limit_bytes=32 << 20),
        cost_estimate=cost(shards * half, keys_num),
        name="second_half",
    )(pattern, valid_rows, start, off_chip(x), off_chip(kv), off_chip(acc))


def join_kernel(z_in, first_ref, last_ref, low_ref, high_ref, z_hbm, sum_ref, sems):
    edge, rows = first_ref.shape[:2]
    shards = z_hbm.shape[0]
    sum_ref[0] = (first_ref[...] + low_ref[...].astype(jnp.float32)).astype(sum_ref.dtype)
    sum_ref[1] = (last_ref[...] + high_ref[...].astype(jnp.float32)).astype(sum_ref.dtype)
    copies = [
        pltpu.make_async_copy(
            sum_ref.at[i], z_hbm.at[pl.ds(at, edge), pl.ds(0, rows)], sems.at[i]
        )
        for i, at in enumerate((0, shards - edge))
    ]
    for copy in copies:
        copy.start()
    for copy in copies:
        copy.wait()


def join_faces(z, first, last, low, high):
    hbm = pl.BlockSpec(memory_space=pltpu.HBM)
    vmem = pl.BlockSpec(memory_space=pltpu.VMEM)
    return pl.pallas_call(
        join_kernel,
        out_shape=pltpu.HBM(z.shape, z.dtype),
        in_specs=[hbm, vmem, vmem, vmem, vmem],
        out_specs=hbm,
        scratch_shapes=[pltpu.VMEM((2, *low.shape), z.dtype), pltpu.SemaphoreType.DMA((2,))],
        input_output_aliases={0: 0},
        compiler_params=pltpu.CompilerParams(vmem_limit_bytes=8 << 20),
        name="join_faces",
    )(z, *(on_chip(a) for a in (first, last, low, high)))


def body(query, key, value, grad_out, pattern, valid_rows):
    def exchange(x):
        return lax.all_to_all(x, "seq", split_axis=0, concat_axis=0, tiled=True)

    size = lax.axis_size("slab")
    up = [(i, i + 1) for i in range(size - 1)]
    down = [(i + 1, i) for i in range(size - 1)]
    rows = query.shape[0]
    edge = FACE * BLOCK // rows
    one, two = pack_heads(key, value, query, grad_out)
    one = exchange(one)
    first, last = take_faces(one, edge, rows)
    before = lax.ppermute(last, "slab", up)
    after = lax.ppermute(first, "slab", down)
    two = exchange(two)
    start = (lax.axis_index("slab") * pattern.shape[0] - FACE).astype(jnp.int32).reshape(1)
    scalars = (pattern.reshape(-1), valid_rows, start)
    od, kv, acc = first_half(*scalars, one, before, after)
    od = exchange(od)
    z, first, last, to_before, to_after = second_half(*scalars, two, kv, acc, edge)
    high = lax.ppermute(to_before, "slab", down)
    low = lax.ppermute(to_after, "slab", up)
    z = exchange(join_faces(z, first, last, low, high))
    grad_key, grad_value, grad_query, attn_out = unpack_heads(z, od)
    return (attn_out, grad_query, grad_key, grad_value)


def solution(mesh):
    rows = P(("slab", "seq"), None)
    return jax.shard_map(
        body,
        mesh=mesh,
        in_specs=(rows, rows, rows, rows, P("slab", None), P()),
        out_specs=(rows, rows, rows, rows),
        check_vma=False,
    )
```

```python
from functools import partial
import math

import jax
import jax.numpy as jnp
from jax import lax
from jax.experimental import pallas as pl
from jax.experimental.pallas import tpu as pltpu
from jax.sharding import PartitionSpec as P

HEAD_DIM = 64
BLOCK = 64
FACE = 16
PAIR = 2 * HEAD_DIM
CHUNKS = 4

score_scale = 0.125
exp2_scale = score_scale * math.log2(math.e)


def on_chip(x):
    return pltpu.with_memory_space_constraint(x, pltpu.VMEM)


def off_chip(x):
    return pltpu.with_memory_space_constraint(x, pltpu.HBM)


def faces_kernel(x_hbm, first_ref, last_ref, sems):
    edge, rows = first_ref.shape[:2]
    copies = [
        pltpu.make_async_copy(x_hbm.at[pl.ds(at, edge), pl.ds(0, rows)], ref, sems.at[i])
        for i, (at, ref) in enumerate(((0, first_ref), (x_hbm.shape[0] - edge, last_ref)))
    ]
    for copy in copies:
        copy.start()
    for copy in copies:
        copy.wait()


def take_faces(x, edge, rows):
    vmem = pl.BlockSpec(memory_space=pltpu.VMEM)
    return pl.pallas_call(
        faces_kernel,
        out_shape=(pltpu.VMEM((edge, rows, PAIR), x.dtype),) * 2,
        in_specs=[pl.BlockSpec(memory_space=pltpu.HBM)],
        out_specs=(vmem, vmem),
        scratch_shapes=[pltpu.SemaphoreType.DMA((2,))],
        compiler_params=pltpu.CompilerParams(vmem_limit_bytes=4 << 20),
        name="take_faces",
    )(off_chip(x))


def swap_halves(a, b):
    low = jnp.concatenate([a[:, :HEAD_DIM], b[:, :HEAD_DIM]], axis=1)
    high = jnp.concatenate([a[:, HEAD_DIM:], b[:, HEAD_DIM:]], axis=1)
    return low, high


def pack_kernel(
    k_hbm, v_hbm, q_hbm, g_hbm, one_hbm, two_hbm, in_refs, out_refs, in_sems, one_sems, two_sems,
):
    rows, half = k_hbm.shape[0], two_hbm.shape[1]
    chunk = rows // CHUNKS
    pairs = ((k_hbm, v_hbm), (q_hbm, g_hbm))

    def span(c):
        return pl.ds(c * chunk, chunk)

    def load(n, i, c):
        return pltpu.make_async_copy(
            pairs[n][i].at[span(c)], in_refs.at[2 * n + i, span(c)], in_sems.at[2 * n + i, c]
        )

    def store(n, c):
        if n == 0 or c * chunk < half:
            target = one_hbm.at[:, pl.ds(n * rows + c * chunk, chunk)]
        else:
            target = two_hbm.at[:, pl.ds(c * chunk - half, chunk)]
        return pltpu.make_async_copy(
            out_refs.at[n, :, span(c)], target, (one_sems if n == 0 else two_sems).at[c]
        )

    order = [(n, c) for n in range(2) for c in range(CHUNKS)]
    for n, c in order:
        for i in range(2):
            load(n, i, c).start()
    for n, c in order:
        for i in range(2):
            load(n, i, c).wait()
        part = slice(c * chunk, (c + 1) * chunk)
        for p in range(k_hbm.shape[1] // PAIR):
            cols = slice(p * PAIR, (p + 1) * PAIR)
            halves = swap_halves(in_refs[2 * n, part, cols], in_refs[2 * n + 1, part, cols])
            out_refs[n, 2 * p, part], out_refs[n, 2 * p + 1, part] = halves
        store(n, c).start()
    for n, c in order:
        store(n, c).wait()


def pack_heads(k, v, q, g):
    rows, cols = k.shape
    heads, half = cols // HEAD_DIM, rows // 2
    hbm = pl.BlockSpec(memory_space=pltpu.HBM)
    return pl.pallas_call(
        pack_kernel,
        out_shape=tuple(pltpu.HBM((heads, size, PAIR), k.dtype) for size in (rows + half, half)),
        in_specs=[hbm] * 4,
        out_specs=(hbm, hbm),
        scratch_shapes=[
            pltpu.VMEM((4, rows, cols), k.dtype),
            pltpu.VMEM((2, heads, rows, PAIR), k.dtype),
            pltpu.SemaphoreType.DMA((4, CHUNKS)),
            pltpu.SemaphoreType.DMA((CHUNKS,)),
            pltpu.SemaphoreType.DMA((CHUNKS,)),
        ],
        compiler_params=pltpu.CompilerParams(vmem_limit_bytes=60 << 20),
        name="pack_heads",
    )(*(off_chip(x) for x in (k, v, q, g)))


def unpack_kernel(
    one_hbm, two_hbm, k_hbm, v_hbm, q_hbm, o_hbm, in_refs, out_refs, one_sems, two_sems, out_sems,
):
    rows, half = k_hbm.shape[0], two_hbm.shape[1]
    chunk = rows // CHUNKS
    pairs = ((k_hbm, v_hbm), (q_hbm, o_hbm))

    def span(c):
        return pl.ds(c * chunk, chunk)

    def load(n, c):
        if n == 0:
            source = one_hbm.at[:, span(c)]
        elif c * chunk < half:
            source = two_hbm.at[:, span(c)]
        else:
            source = one_hbm.at[:, pl.ds(rows + c * chunk - half, chunk)]
        return pltpu.make_async_copy(
            source, in_refs.at[n, :, span(c)], (one_sems if n == 0 else two_sems).at[c]
        )

    def store(n, i, c):
        return pltpu.make_async_copy(
            out_refs.at[2 * n + i, span(c)], pairs[n][i].at[span(c)], out_sems.at[2 * n + i, c]
        )

    order = [(n, c) for n in range(2) for c in range(CHUNKS)]
    for n, c in order:
        load(n, c).start()
    for n, c in order:
        load(n, c).wait()
        part = slice(c * chunk, (c + 1) * chunk)
        for p in range(k_hbm.shape[1] // PAIR):
            cols = slice(p * PAIR, (p + 1) * PAIR)
            halves = swap_halves(in_refs[n, 2 * p, part], in_refs[n, 2 * p + 1, part])
            out_refs[2 * n, part, cols], out_refs[2 * n + 1, part, cols] = halves
        for i in range(2):
            store(n, i, c).start()
    for n, c in order:
        for i in range(2):
            store(n, i, c).wait()


def unpack_heads(one, two):
    heads, half, _ = two.shape
    rows, cols = 2 * half, heads * HEAD_DIM
    hbm = pl.BlockSpec(memory_space=pltpu.HBM)
    return pl.pallas_call(
        unpack_kernel,
        out_shape=(pltpu.HBM((rows, cols), one.dtype),) * 4,
        in_specs=[hbm, hbm],
        out_specs=(hbm,) * 4,
        scratch_shapes=[
            pltpu.VMEM((2, heads, rows, PAIR), one.dtype),
            pltpu.VMEM((4, rows, cols), one.dtype),
            pltpu.SemaphoreType.DMA((CHUNKS,)),
            pltpu.SemaphoreType.DMA((CHUNKS,)),
            pltpu.SemaphoreType.DMA((4, CHUNKS)),
        ],
        compiler_params=pltpu.CompilerParams(vmem_limit_bytes=60 << 20),
        name="unpack_heads",
    )(off_chip(one), off_chip(two))


def in_turn(*tasks):
    def steps(stage, blocks):
        for u in blocks:
            yield from stage(u)

    running = [steps(*task) for task in tasks]
    while running:
        running = [task for task in running if next(task, True) is None]


def query_blocks(
    pattern_ref, valid_ref, start_ref, kv_ref, qg_ref, acc_ref, od_ref, both_ref, pd_ref, send_od,
    *, keys_num, chunk, group, lines, ready=None,
):
    shards, rows = qg_ref.shape[:2]
    each = rows // BLOCK
    start = start_ref[0]
    low = lax.broadcasted_iota(jnp.int32, (BLOCK, PAIR), 1) < HEAD_DIM
    lane = lax.broadcasted_iota(jnp.int32, (1, PAIR), 1)

    def one_group(t, _):
        shard = t * (group // each)
        meta = []
        for u in range(group):
            s, i = u // each, u % each
            base = ((shard + s) * 2 * each + chunk * each + i) * keys_num
            slots = [pattern_ref[base + j] for j in range(keys_num)]
            counts = [valid_ref[start + slot] for slot in slots]
            meta.append((s, slice(i * BLOCK, (i + 1) * BLOCK), slots, counts))

        def gathered(slots):
            return jnp.concatenate(
                [kv_ref[pl.ds(pl.multiple_of(slot * BLOCK, BLOCK), BLOCK), :] for slot in slots],
                axis=0,
            )

        def spread(s, part):
            qg = qg_ref[shard + s, part, :]
            zero = jnp.zeros_like(qg)
            return jnp.concatenate([jnp.where(low, zero, qg), jnp.where(low, qg, zero)], axis=0)

        def probe(u):
            s, part, slots, counts = meta[u]
            kv, gq = gathered(slots), spread(s, part)
            for n in range(0, keys_num * BLOCK, 2 * PAIR):
                both_ref[u, :, n : n + 2 * PAIR] = lax.dot_general(
                    gq, kv[n : n + 2 * PAIR], (((1,), (1,)), ((), ())),
                    preferred_element_type=jnp.float32,
                )
                yield

        def weigh(u):
            s, part, slots, counts = meta[u]
            bias = jnp.concatenate(
                [
                    jnp.where(
                        lane < jnp.where(lane < HEAD_DIM, counts[j], counts[j + 1] + HEAD_DIM),
                        0.0,
                        -jnp.inf,
                    )
                    for j in range(0, keys_num, 2)
                ],
                axis=1,
            )
            for r in range(0, BLOCK, lines):
                scores = both_ref[u, BLOCK + r : BLOCK + r + lines, :] + bias
                top = jnp.max(scores, axis=1, keepdims=True)
                weight = jnp.exp2((scores - top) * exp2_scale)
                total = jnp.sum(weight, axis=1, keepdims=True)
                prob = (weight * (1.0 / total)).astype(jnp.bfloat16)
                prob_wide = prob.astype(jnp.float32)
                grad_prob = both_ref[u, r : r + lines, :]
                delta = jnp.sum(prob_wide * grad_prob, axis=1, keepdims=True)
                dscore = (prob_wide * (grad_prob - delta)).astype(jnp.bfloat16)
                pd_ref[u, r : r + lines, :] = prob
                pd_ref[u, BLOCK + r : BLOCK + r + lines, :] = dscore
                yield

        def rows_out(u):
            s, part, slots, counts = meta[u]
            od = jnp.dot(pd_ref[u], gathered(slots), preferred_element_type=jnp.float32)
            od_ref[shard + s, part, :] = jnp.where(
                low, od[BLOCK:] * score_scale, od[:BLOCK]
            ).astype(od_ref.dtype)
            yield

        def keys_out(u):
            s, part, slots, counts = meta[u]
            dkv = lax.dot_general(
                pd_ref[u], spread(s, part), (((0,), (0,)), ((), ())),
                preferred_element_type=jnp.float32,
            )
            yield
            for j, slot in enumerate(slots):
                span = pl.ds(pl.multiple_of(slot * BLOCK, BLOCK), BLOCK)
                acc_ref[span, :] += dkv[j * BLOCK : (j + 1) * BLOCK]
                if j % 2:
                    yield

        near, far = range(group // 2), range(group // 2, group)
        in_turn((probe, near))
        in_turn((probe, far), (weigh, near))
        if ready is not None:
            pl.when(t == 0)(ready)
        in_turn((keys_out, near), (weigh, far))
        in_turn((rows_out, range(group)))
        for s in range(group // each):
            send_od(shard + s).start()
        in_turn((keys_out, far))
        return 0

    lax.fori_loop(0, shards * each // group, one_group, 0)


def first_kernel(
    pattern_ref, valid_ref, start_ref, x_hbm, before_ref, after_ref,
    od_hbm, kv_hbm, acc_hbm,
    kv_ref, acc_ref, qg_ref, od_ref, both_ref, pd_ref, in_sems, od_sems, out_sems, **sizes,
):
    shards, half = qg_ref.shape[:2]
    rows = x_hbm.shape[1] - half
    edge = before_ref.shape[0]

    def fetch(source, i):
        return pltpu.make_async_copy(source, kv_ref.at[pl.ds(i * rows, rows)], in_sems.at[i])

    copies = [fetch(x_hbm.at[t, pl.ds(0, rows)], edge + t) for t in range(shards)]
    copies += [fetch(before_ref.at[t], t) for t in range(edge)]
    copies += [fetch(after_ref.at[t], edge + shards + t) for t in range(edge)]
    copies += [
        pltpu.make_async_copy(x_hbm.at[:, pl.ds(rows, half)], qg_ref, in_sems.at[len(copies)])
    ]
    for copy in copies:
        copy.start()
    acc_ref[...] = jnp.zeros_like(acc_ref)
    for copy in copies:
        copy.wait()
    keep = pltpu.make_async_copy(kv_ref, kv_hbm, out_sems.at[0])
    keep.start()

    def send_od(t):
        return pltpu.make_async_copy(od_ref.at[t], od_hbm.at[t], od_sems.at[t])

    query_blocks(
        pattern_ref, valid_ref, start_ref, kv_ref, qg_ref, acc_ref, od_ref, both_ref, pd_ref,
        send_od, chunk=0, **sizes,
    )
    total = pltpu.make_async_copy(acc_ref, acc_hbm, out_sems.at[1])
    total.start()
    for t in range(shards):
        send_od(t).wait()
    keep.wait()
    total.wait()


def second_kernel(
    pattern_ref, valid_ref, start_ref, x_hbm, kv_hbm, acc_hbm,
    z_hbm, first_ref, last_ref, down_ref, up_ref,
    kv_ref, acc_ref, qg_ref, od_ref, dkv_ref, both_ref, pd_ref, in_sems, od_sems, dkv_sems, **sizes,
):
    shards, half = qg_ref.shape[:2]
    rows = 2 * half
    edge = first_ref.shape[0]
    copies = [
        pltpu.make_async_copy(source, target, in_sems.at[i])
        for i, (source, target) in enumerate(((x_hbm, qg_ref), (kv_hbm, kv_ref), (acc_hbm, acc_ref)))
    ]
    for copy in copies:
        copy.start()
    copies[0].wait()
    copies[1].wait()

    def send_od(t):
        return pltpu.make_async_copy(od_ref.at[t], z_hbm.at[t, pl.ds(rows, half)], od_sems.at[t])

    def send_dkv(t):
        return pltpu.make_async_copy(dkv_ref.at[t], z_hbm.at[t, pl.ds(0, rows)], dkv_sems.at[t])

    query_blocks(
        pattern_ref, valid_ref, start_ref, kv_ref, qg_ref, acc_ref, od_ref, both_ref, pd_ref,
        send_od, chunk=1, ready=copies[2].wait, **sizes,
    )
    low = lax.broadcasted_iota(jnp.int32, (rows, PAIR), 1) < HEAD_DIM

    def scaled(s):
        tile = acc_ref[s * rows : (s + 1) * rows, :]
        return jnp.where(low, tile * score_scale, tile)

    for t in range(edge, shards - edge):
        dkv_ref[t] = scaled(edge + t).astype(dkv_ref.dtype)
        send_dkv(t).start()
    for s in range(edge):
        down_ref[s] = scaled(s).astype(down_ref.dtype)
        up_ref[s] = scaled(edge + shards + s).astype(up_ref.dtype)
        first_ref[s] = scaled(edge + s)
        last_ref[s] = scaled(shards + s)
    for t in range(shards):
        send_od(t).wait()
    for t in range(edge, shards - edge):
        send_dkv(t).wait()


def cost(tokens, keys_num):
    work = tokens * keys_num * BLOCK
    return pl.CostEstimate(flops=12 * PAIR * work, transcendentals=work, bytes_accessed=16 << 20)


def first_half(pattern, valid_rows, start, x, before, after, group=16, lines=16):
    keys_num = pattern.shape[0] * BLOCK // (x.shape[0] * before.shape[1])
    shards, edge, rows = x.shape[0], before.shape[0], before.shape[1]
    half, ext = rows // 2, shards + 2 * edge
    smem = pl.BlockSpec(memory_space=pltpu.SMEM)
    hbm = pl.BlockSpec(memory_space=pltpu.HBM)
    vmem = pl.BlockSpec(memory_space=pltpu.VMEM)
    return pl.pallas_call(
        partial(first_kernel, keys_num=keys_num, group=group, lines=lines),
        out_shape=(
            pltpu.HBM((shards, half, PAIR), x.dtype),
            pltpu.HBM((ext * rows, PAIR), x.dtype),
            pltpu.HBM((ext * rows, PAIR), jnp.float32),
        ),
        in_specs=[smem, smem, smem, hbm, vmem, vmem],
        out_specs=(hbm, hbm, hbm),
        scratch_shapes=[
            pltpu.VMEM((ext * rows, PAIR), x.dtype),
            pltpu.VMEM((ext * rows, PAIR), jnp.float32),
            pltpu.VMEM((shards, half, PAIR), x.dtype),
            pltpu.VMEM((shards, half, PAIR), x.dtype),
            pltpu.VMEM((group, PAIR, keys_num * BLOCK), jnp.float32),
            pltpu.VMEM((group, PAIR, keys_num * BLOCK), x.dtype),
            pltpu.SemaphoreType.DMA((ext + 1,)),
            pltpu.SemaphoreType.DMA((shards,)),
            pltpu.SemaphoreType.DMA((2,)),
        ],
        compiler_params=pltpu.CompilerParams(vmem_limit_bytes=32 << 20),
        cost_estimate=cost(shards * half, keys_num),
        name="first_half",
    )(pattern, valid_rows, start, off_chip(x), on_chip(before), on_chip(after))


def second_half(pattern, valid_rows, start, x, kv, acc, edge, group=16, lines=16):
    shards, half = x.shape[:2]
    rows = 2 * half
    keys_num = pattern.shape[0] * BLOCK // (shards * rows)
    smem = pl.BlockSpec(memory_space=pltpu.SMEM)
    hbm = pl.BlockSpec(memory_space=pltpu.HBM)
    vmem = pl.BlockSpec(memory_space=pltpu.VMEM)
    face = (edge, rows, PAIR)
    return pl.pallas_call(
        partial(second_kernel, keys_num=keys_num, group=group, lines=lines),
        out_shape=(pltpu.HBM((shards, rows + half, PAIR), x.dtype),)
        + (pltpu.VMEM(face, jnp.float32),) * 2
        + (pltpu.VMEM(face, x.dtype),) * 2,
        in_specs=[smem, smem, smem, hbm, hbm, hbm],
        out_specs=(hbm, vmem, vmem, vmem, vmem),
        scratch_shapes=[
            pltpu.VMEM(kv.shape, kv.dtype),
            pltpu.VMEM(acc.shape, acc.dtype),
            pltpu.VMEM((shards, half, PAIR), x.dtype),
            pltpu.VMEM((shards, half, PAIR), x.dtype),
            pltpu.VMEM((shards, rows, PAIR), x.dtype),
            pltpu.VMEM((group, PAIR, keys_num * BLOCK), jnp.float32),
            pltpu.VMEM((group, PAIR, keys_num * BLOCK), x.dtype),
            pltpu.SemaphoreType.DMA((3,)),
            pltpu.SemaphoreType.DMA((shards,)),
            pltpu.SemaphoreType.DMA((shards,)),
        ],
        compiler_params=pltpu.CompilerParams(vmem_limit_bytes=32 << 20),
        cost_estimate=cost(shards * half, keys_num),
        name="second_half",
    )(pattern, valid_rows, start, off_chip(x), off_chip(kv), off_chip(acc))


def join_kernel(z_in, first_ref, last_ref, low_ref, high_ref, z_hbm, sum_ref, sems):
    edge, rows = first_ref.shape[:2]
    shards = z_hbm.shape[0]
    sum_ref[0] = (first_ref[...] + low_ref[...].astype(jnp.float32)).astype(sum_ref.dtype)
    sum_ref[1] = (last_ref[...] + high_ref[...].astype(jnp.float32)).astype(sum_ref.dtype)
    copies = [
        pltpu.make_async_copy(
            sum_ref.at[i], z_hbm.at[pl.ds(at, edge), pl.ds(0, rows)], sems.at[i]
        )
        for i, at in enumerate((0, shards - edge))
    ]
    for copy in copies:
        copy.start()
    for copy in copies:
        copy.wait()


def join_faces(z, first, last, low, high):
    hbm = pl.BlockSpec(memory_space=pltpu.HBM)
    vmem = pl.BlockSpec(memory_space=pltpu.VMEM)
    return pl.pallas_call(
        join_kernel,
        out_shape=pltpu.HBM(z.shape, z.dtype),
        in_specs=[hbm, vmem, vmem, vmem, vmem],
        out_specs=hbm,
        scratch_shapes=[pltpu.VMEM((2, *low.shape), z.dtype), pltpu.SemaphoreType.DMA((2,))],
        input_output_aliases={0: 0},
        compiler_params=pltpu.CompilerParams(vmem_limit_bytes=8 << 20),
        name="join_faces",
    )(z, *(on_chip(a) for a in (first, last, low, high)))


def body(query, key, value, grad_out, pattern, valid_rows):
    def exchange(x):
        return lax.all_to_all(x, "seq", split_axis=0, concat_axis=0, tiled=True)

    size = lax.axis_size("slab")
    up = [(i, i + 1) for i in range(size - 1)]
    down = [(i + 1, i) for i in range(size - 1)]
    rows = query.shape[0]
    edge = FACE * BLOCK // rows
    one, two = pack_heads(key, value, query, grad_out)
    one = exchange(one)
    first, last = take_faces(one, edge, rows)
    before = lax.ppermute(last, "slab", up)
    after = lax.ppermute(first, "slab", down)
    before, two = lax.optimization_barrier((before, two))
    two = exchange(two)
    start = (lax.axis_index("slab") * pattern.shape[0] - FACE).astype(jnp.int32).reshape(1)
    scalars = (pattern.reshape(-1), valid_rows, start)
    od, kv, acc = first_half(*scalars, one, before, after)
    od = exchange(od)
    z, first, last, to_before, to_after = second_half(*scalars, two, kv, acc, edge)
    high = lax.ppermute(to_before, "slab", down)
    low = lax.ppermute(to_after, "slab", up)
    z = exchange(join_faces(z, first, last, low, high))
    grad_key, grad_value, grad_query, attn_out = unpack_heads(z, od)
    return (attn_out, grad_query, grad_key, grad_value)


def solution(mesh):
    rows = P(("slab", "seq"), None)
    return jax.shard_map(
        body,
        mesh=mesh,
        in_specs=(rows, rows, rows, rows, P("slab", None), P()),
        out_specs=(rows, rows, rows, rows),
        check_vma=False,
    )
```

```python
from functools import partial
import math

import jax
import jax.numpy as jnp
from jax import lax
from jax.experimental import pallas as pl
from jax.experimental.pallas import tpu as pltpu
from jax.sharding import PartitionSpec as P

HEAD_DIM = 64
BLOCK = 64
FACE = 16
PAIR = 2 * HEAD_DIM
CHUNKS = 4

score_scale = 0.125
exp2_scale = score_scale * math.log2(math.e)


def on_chip(x):
    return pltpu.with_memory_space_constraint(x, pltpu.VMEM)


def off_chip(x):
    return pltpu.with_memory_space_constraint(x, pltpu.HBM)


def faces_kernel(x_hbm, first_ref, last_ref, sems):
    edge, rows = first_ref.shape[:2]
    copies = [
        pltpu.make_async_copy(x_hbm.at[pl.ds(at, edge), pl.ds(0, rows)], ref, sems.at[i])
        for i, (at, ref) in enumerate(((0, first_ref), (x_hbm.shape[0] - edge, last_ref)))
    ]
    for copy in copies:
        copy.start()
    for copy in copies:
        copy.wait()


def take_faces(x, edge, rows):
    vmem = pl.BlockSpec(memory_space=pltpu.VMEM)
    return pl.pallas_call(
        faces_kernel,
        out_shape=(pltpu.VMEM((edge, rows, PAIR), x.dtype),) * 2,
        in_specs=[pl.BlockSpec(memory_space=pltpu.HBM)],
        out_specs=(vmem, vmem),
        scratch_shapes=[pltpu.SemaphoreType.DMA((2,))],
        compiler_params=pltpu.CompilerParams(vmem_limit_bytes=4 << 20),
        name="take_faces",
    )(off_chip(x))


def swap_halves(a, b):
    low = jnp.concatenate([a[:, :HEAD_DIM], b[:, :HEAD_DIM]], axis=1)
    high = jnp.concatenate([a[:, HEAD_DIM:], b[:, HEAD_DIM:]], axis=1)
    return low, high


def pack_kernel(
    k_hbm, v_hbm, q_hbm, g_hbm, one_hbm, two_hbm, in_refs, out_refs, in_sems, one_sems, two_sems,
):
    rows, half = k_hbm.shape[0], two_hbm.shape[1]
    chunk = rows // CHUNKS
    pairs = ((k_hbm, v_hbm), (q_hbm, g_hbm))

    def span(c):
        return pl.ds(c * chunk, chunk)

    def load(n, i, c):
        return pltpu.make_async_copy(
            pairs[n][i].at[span(c)], in_refs.at[2 * n + i, span(c)], in_sems.at[2 * n + i, c]
        )

    def store(n, c):
        if n == 0 or c * chunk < half:
            target = one_hbm.at[:, pl.ds(n * rows + c * chunk, chunk)]
        else:
            target = two_hbm.at[:, pl.ds(c * chunk - half, chunk)]
        return pltpu.make_async_copy(
            out_refs.at[n, :, span(c)], target, (one_sems if n == 0 else two_sems).at[c]
        )

    order = [(n, c) for n in range(2) for c in range(CHUNKS)]
    for n, c in order:
        for i in range(2):
            load(n, i, c).start()
    for n, c in order:
        for i in range(2):
            load(n, i, c).wait()
        part = slice(c * chunk, (c + 1) * chunk)
        for p in range(k_hbm.shape[1] // PAIR):
            cols = slice(p * PAIR, (p + 1) * PAIR)
            halves = swap_halves(in_refs[2 * n, part, cols], in_refs[2 * n + 1, part, cols])
            out_refs[n, 2 * p, part], out_refs[n, 2 * p + 1, part] = halves
        store(n, c).start()
    for n, c in order:
        store(n, c).wait()


def pack_heads(k, v, q, g):
    rows, cols = k.shape
    heads, half = cols // HEAD_DIM, rows // 2
    hbm = pl.BlockSpec(memory_space=pltpu.HBM)
    return pl.pallas_call(
        pack_kernel,
        out_shape=tuple(pltpu.HBM((heads, size, PAIR), k.dtype) for size in (rows + half, half)),
        in_specs=[hbm] * 4,
        out_specs=(hbm, hbm),
        scratch_shapes=[
            pltpu.VMEM((4, rows, cols), k.dtype),
            pltpu.VMEM((2, heads, rows, PAIR), k.dtype),
            pltpu.SemaphoreType.DMA((4, CHUNKS)),
            pltpu.SemaphoreType.DMA((CHUNKS,)),
            pltpu.SemaphoreType.DMA((CHUNKS,)),
        ],
        compiler_params=pltpu.CompilerParams(vmem_limit_bytes=60 << 20),
        name="pack_heads",
    )(*(off_chip(x) for x in (k, v, q, g)))


def chunks(source, row, size, to, chunk):
    return [(source, row + i, chunk, to + i) for i in range(0, size, chunk)]


def unpack_kernel(*refs, jobs, count, skip):
    source, targets = refs[0], refs[1 + skip : 1 + skip + count]
    out_refs, sems = refs[1 + skip + count :]

    def store(n, i):
        target, row, size, at = jobs[n]
        return pltpu.make_async_copy(
            out_refs.at[i, pl.ds(at, size)], targets[target + i].at[pl.ds(row, size)], sems.at[i, n]
        )

    for n, (_, _, size, at) in enumerate(jobs):
        part = slice(at, at + size)
        for p in range(source.shape[0] // 2):
            cols = slice(p * PAIR, (p + 1) * PAIR)
            halves = swap_halves(source[2 * p, part], source[2 * p + 1, part])
            out_refs[0, part, cols], out_refs[1, part, cols] = halves
        for i in range(2):
            store(n, i).start()
    for n in range(len(jobs)):
        for i in range(2):
            store(n, i).wait()


def unpack_heads(x, full_rows, jobs, count, name, into=()):
    heads, rows, _ = x.shape
    cols = heads * HEAD_DIM
    hbm = pl.BlockSpec(memory_space=pltpu.HBM)
    return pl.pallas_call(
        partial(unpack_kernel, jobs=jobs, count=count, skip=len(into)),
        out_shape=(pltpu.HBM((full_rows, cols), x.dtype),) * count,
        in_specs=[pl.BlockSpec(memory_space=pltpu.VMEM)] + [hbm] * len(into),
        out_specs=(hbm,) * count,
        scratch_shapes=[
            pltpu.VMEM((2, rows, cols), x.dtype),
            pltpu.SemaphoreType.DMA((2, len(jobs))),
        ],
        input_output_aliases={1 + i: count - len(into) + i for i in range(len(into))},
        compiler_params=pltpu.CompilerParams(vmem_limit_bytes=16 << 20),
        cost_estimate=pl.CostEstimate(
            flops=0, transcendentals=0, bytes_accessed=4 * rows * cols * x.dtype.itemsize
        ),
        name=name,
    )(on_chip(x), *(off_chip(a) for a in into))


def in_turn(*tasks):
    def steps(stage, blocks):
        for u in blocks:
            yield from stage(u)

    running = [steps(*task) for task in tasks]
    while running:
        running = [task for task in running if next(task, True) is None]


def query_blocks(
    pattern_ref, valid_ref, start_ref, kv_ref, qg_ref, acc_ref, od_ref, both_ref, pd_ref, send_od,
    *, keys_num, chunk, group, lines, ready=None,
):
    shards, rows = qg_ref.shape[:2]
    each = rows // BLOCK
    start = start_ref[0]
    low = lax.broadcasted_iota(jnp.int32, (BLOCK, PAIR), 1) < HEAD_DIM
    lane = lax.broadcasted_iota(jnp.int32, (1, PAIR), 1)

    def one_group(t, _):
        shard = t * (group // each)
        meta = []
        for u in range(group):
            s, i = u // each, u % each
            base = ((shard + s) * 2 * each + chunk * each + i) * keys_num
            slots = [pattern_ref[base + j] for j in range(keys_num)]
            counts = [valid_ref[start + slot] for slot in slots]
            meta.append((s, slice(i * BLOCK, (i + 1) * BLOCK), slots, counts))

        def gathered(slots):
            return jnp.concatenate(
                [kv_ref[pl.ds(pl.multiple_of(slot * BLOCK, BLOCK), BLOCK), :] for slot in slots],
                axis=0,
            )

        def spread(s, part):
            qg = qg_ref[shard + s, part, :]
            zero = jnp.zeros_like(qg)
            return jnp.concatenate([jnp.where(low, zero, qg), jnp.where(low, qg, zero)], axis=0)

        def probe(u):
            s, part, slots, counts = meta[u]
            kv, gq = gathered(slots), spread(s, part)
            for n in range(0, keys_num * BLOCK, 2 * PAIR):
                both_ref[u, :, n : n + 2 * PAIR] = lax.dot_general(
                    gq, kv[n : n + 2 * PAIR], (((1,), (1,)), ((), ())),
                    preferred_element_type=jnp.float32,
                )
                yield

        def weigh(u):
            s, part, slots, counts = meta[u]
            bias = jnp.concatenate(
                [
                    jnp.where(
                        lane < jnp.where(lane < HEAD_DIM, counts[j], counts[j + 1] + HEAD_DIM),
                        0.0,
                        -jnp.inf,
                    )
                    for j in range(0, keys_num, 2)
                ],
                axis=1,
            )
            for r in range(0, BLOCK, lines):
                scores = both_ref[u, BLOCK + r : BLOCK + r + lines, :] + bias
                top = jnp.max(scores, axis=1, keepdims=True)
                weight = jnp.exp2((scores - top) * exp2_scale)
                total = jnp.sum(weight, axis=1, keepdims=True)
                prob = (weight * (1.0 / total)).astype(jnp.bfloat16)
                prob_wide = prob.astype(jnp.float32)
                grad_prob = both_ref[u, r : r + lines, :]
                delta = jnp.sum(prob_wide * grad_prob, axis=1, keepdims=True)
                dscore = (prob_wide * (grad_prob - delta)).astype(jnp.bfloat16)
                pd_ref[u, r : r + lines, :] = prob
                pd_ref[u, BLOCK + r : BLOCK + r + lines, :] = dscore
                yield

        def rows_out(u):
            s, part, slots, counts = meta[u]
            od = jnp.dot(pd_ref[u], gathered(slots), preferred_element_type=jnp.float32)
            od_ref[shard + s, part, :] = jnp.where(
                low, od[BLOCK:] * score_scale, od[:BLOCK]
            ).astype(od_ref.dtype)
            yield

        def keys_out(u):
            s, part, slots, counts = meta[u]
            dkv = lax.dot_general(
                pd_ref[u], spread(s, part), (((0,), (0,)), ((), ())),
                preferred_element_type=jnp.float32,
            )
            yield
            for j, slot in enumerate(slots):
                span = pl.ds(pl.multiple_of(slot * BLOCK, BLOCK), BLOCK)
                acc_ref[span, :] += dkv[j * BLOCK : (j + 1) * BLOCK]
                if j % 2:
                    yield

        near, far = range(group // 2), range(group // 2, group)
        in_turn((probe, near))
        in_turn((probe, far), (weigh, near))
        if ready is not None:
            pl.when(t == 0)(ready)
        in_turn((keys_out, near), (weigh, far))
        in_turn((rows_out, range(group)))
        for s in range(group // each):
            send_od(shard + s).start()
        in_turn((keys_out, far))
        return 0

    lax.fori_loop(0, shards * each // group, one_group, 0)


def first_kernel(
    pattern_ref, valid_ref, start_ref, x_hbm, before_ref, after_ref,
    od_hbm, kv_hbm, acc_hbm,
    kv_ref, acc_ref, qg_ref, od_ref, both_ref, pd_ref, in_sems, od_sems, out_sems, **sizes,
):
    shards, half = qg_ref.shape[:2]
    rows = x_hbm.shape[1] - half
    edge = before_ref.shape[0]

    def fetch(source, i):
        return pltpu.make_async_copy(source, kv_ref.at[pl.ds(i * rows, rows)], in_sems.at[i])

    copies = [fetch(x_hbm.at[t, pl.ds(0, rows)], edge + t) for t in range(shards)]
    copies += [fetch(before_ref.at[t], t) for t in range(edge)]
    copies += [fetch(after_ref.at[t], edge + shards + t) for t in range(edge)]
    copies += [
        pltpu.make_async_copy(x_hbm.at[:, pl.ds(rows, half)], qg_ref, in_sems.at[len(copies)])
    ]
    for copy in copies:
        copy.start()
    acc_ref[...] = jnp.zeros_like(acc_ref)
    for copy in copies:
        copy.wait()
    keep = pltpu.make_async_copy(kv_ref, kv_hbm, out_sems.at[0])
    keep.start()

    def send_od(t):
        return pltpu.make_async_copy(od_ref.at[t], od_hbm.at[t], od_sems.at[t])

    query_blocks(
        pattern_ref, valid_ref, start_ref, kv_ref, qg_ref, acc_ref, od_ref, both_ref, pd_ref,
        send_od, chunk=0, **sizes,
    )
    total = pltpu.make_async_copy(acc_ref, acc_hbm, out_sems.at[1])
    total.start()
    for t in range(shards):
        send_od(t).wait()
    keep.wait()
    total.wait()


def second_kernel(
    pattern_ref, valid_ref, start_ref, qg_ref, kv_hbm, acc_hbm,
    z_hbm, first_ref, last_ref, down_ref, up_ref,
    kv_ref, acc_ref, od_ref, dkv_ref, both_ref, pd_ref, in_sems, od_sems, dkv_sems, **sizes,
):
    shards, half = qg_ref.shape[:2]
    rows = 2 * half
    edge = first_ref.shape[0]
    copies = [
        pltpu.make_async_copy(source, target, in_sems.at[i])
        for i, (source, target) in enumerate(((kv_hbm, kv_ref), (acc_hbm, acc_ref)))
    ]
    for copy in copies:
        copy.start()
    copies[0].wait()

    def send_od(t):
        return pltpu.make_async_copy(od_ref.at[t], z_hbm.at[t, pl.ds(rows, half)], od_sems.at[t])

    def send_dkv(t):
        return pltpu.make_async_copy(dkv_ref.at[t], z_hbm.at[t, pl.ds(0, rows)], dkv_sems.at[t])

    query_blocks(
        pattern_ref, valid_ref, start_ref, kv_ref, qg_ref, acc_ref, od_ref, both_ref, pd_ref,
        send_od, chunk=1, ready=copies[1].wait, **sizes,
    )
    low = lax.broadcasted_iota(jnp.int32, (rows, PAIR), 1) < HEAD_DIM

    def scaled(s):
        tile = acc_ref[s * rows : (s + 1) * rows, :]
        return jnp.where(low, tile * score_scale, tile)

    for t in range(edge, shards - edge):
        dkv_ref[t] = scaled(edge + t).astype(dkv_ref.dtype)
        send_dkv(t).start()
    for s in range(edge):
        down_ref[s] = scaled(s).astype(down_ref.dtype)
        up_ref[s] = scaled(edge + shards + s).astype(up_ref.dtype)
        first_ref[s] = scaled(edge + s)
        last_ref[s] = scaled(shards + s)
    for t in range(shards):
        send_od(t).wait()
    for t in range(edge, shards - edge):
        send_dkv(t).wait()


def cost(tokens, keys_num):
    work = tokens * keys_num * BLOCK
    return pl.CostEstimate(flops=12 * PAIR * work, transcendentals=work, bytes_accessed=16 << 20)


def first_half(pattern, valid_rows, start, x, before, after, group=32, lines=16):
    keys_num = pattern.shape[0] * BLOCK // (x.shape[0] * before.shape[1])
    shards, edge, rows = x.shape[0], before.shape[0], before.shape[1]
    half, ext = rows // 2, shards + 2 * edge
    smem = pl.BlockSpec(memory_space=pltpu.SMEM)
    hbm = pl.BlockSpec(memory_space=pltpu.HBM)
    vmem = pl.BlockSpec(memory_space=pltpu.VMEM)
    return pl.pallas_call(
        partial(first_kernel, keys_num=keys_num, group=group, lines=lines),
        out_shape=(
            pltpu.HBM((shards, half, PAIR), x.dtype),
            pltpu.HBM((ext * rows, PAIR), x.dtype),
            pltpu.HBM((ext * rows, PAIR), jnp.float32),
        ),
        in_specs=[smem, smem, smem, hbm, vmem, vmem],
        out_specs=(hbm, hbm, hbm),
        scratch_shapes=[
            pltpu.VMEM((ext * rows, PAIR), x.dtype),
            pltpu.VMEM((ext * rows, PAIR), jnp.float32),
            pltpu.VMEM((shards, half, PAIR), x.dtype),
            pltpu.VMEM((shards, half, PAIR), x.dtype),
            pltpu.VMEM((group, PAIR, keys_num * BLOCK), jnp.float32),
            pltpu.VMEM((group, PAIR, keys_num * BLOCK), x.dtype),
            pltpu.SemaphoreType.DMA((ext + 1,)),
            pltpu.SemaphoreType.DMA((shards,)),
            pltpu.SemaphoreType.DMA((2,)),
        ],
        compiler_params=pltpu.CompilerParams(vmem_limit_bytes=32 << 20),
        cost_estimate=cost(shards * half, keys_num),
        name="first_half",
    )(pattern, valid_rows, start, off_chip(x), on_chip(before), on_chip(after))


def second_half(pattern, valid_rows, start, x, kv, acc, edge, group=32, lines=16):
    shards, half = x.shape[:2]
    rows = 2 * half
    keys_num = pattern.shape[0] * BLOCK // (shards * rows)
    smem = pl.BlockSpec(memory_space=pltpu.SMEM)
    hbm = pl.BlockSpec(memory_space=pltpu.HBM)
    vmem = pl.BlockSpec(memory_space=pltpu.VMEM)
    face = (edge, rows, PAIR)
    return pl.pallas_call(
        partial(second_kernel, keys_num=keys_num, group=group, lines=lines),
        out_shape=(pltpu.HBM((shards, rows + half, PAIR), x.dtype),)
        + (pltpu.VMEM(face, jnp.float32),) * 2
        + (pltpu.VMEM(face, x.dtype),) * 2,
        in_specs=[smem, smem, smem, vmem, hbm, hbm],
        out_specs=(hbm, vmem, vmem, vmem, vmem),
        scratch_shapes=[
            pltpu.VMEM(kv.shape, kv.dtype),
            pltpu.VMEM(acc.shape, acc.dtype),
            pltpu.VMEM((shards, half, PAIR), x.dtype),
            pltpu.VMEM((shards, rows, PAIR), x.dtype),
            pltpu.VMEM((group, PAIR, keys_num * BLOCK), jnp.float32),
            pltpu.VMEM((group, PAIR, keys_num * BLOCK), x.dtype),
            pltpu.SemaphoreType.DMA((2,)),
            pltpu.SemaphoreType.DMA((shards,)),
            pltpu.SemaphoreType.DMA((shards,)),
        ],
        compiler_params=pltpu.CompilerParams(vmem_limit_bytes=32 << 20),
        cost_estimate=cost(shards * half, keys_num),
        name="second_half",
    )(pattern, valid_rows, start, on_chip(x), off_chip(kv), off_chip(acc))


def join_kernel(z_in, first_ref, last_ref, low_ref, high_ref, z_hbm, sum_ref, sems):
    edge, rows = first_ref.shape[:2]
    shards = z_hbm.shape[0]
    sum_ref[0] = (first_ref[...] + low_ref[...].astype(jnp.float32)).astype(sum_ref.dtype)
    sum_ref[1] = (last_ref[...] + high_ref[...].astype(jnp.float32)).astype(sum_ref.dtype)
    copies = [
        pltpu.make_async_copy(
            sum_ref.at[i], z_hbm.at[pl.ds(at, edge), pl.ds(0, rows)], sems.at[i]
        )
        for i, at in enumerate((0, shards - edge))
    ]
    for copy in copies:
        copy.start()
    for copy in copies:
        copy.wait()


def join_faces(z, first, last, low, high):
    hbm = pl.BlockSpec(memory_space=pltpu.HBM)
    vmem = pl.BlockSpec(memory_space=pltpu.VMEM)
    return pl.pallas_call(
        join_kernel,
        out_shape=pltpu.HBM(z.shape, z.dtype),
        in_specs=[hbm, vmem, vmem, vmem, vmem],
        out_specs=hbm,
        scratch_shapes=[pltpu.VMEM((2, *low.shape), z.dtype), pltpu.SemaphoreType.DMA((2,))],
        input_output_aliases={0: 0},
        compiler_params=pltpu.CompilerParams(vmem_limit_bytes=8 << 20),
        name="join_faces",
    )(z, *(on_chip(a) for a in (first, last, low, high)))


def body(query, key, value, grad_out, pattern, valid_rows):
    def exchange(x):
        return lax.all_to_all(x, "seq", split_axis=0, concat_axis=0, tiled=True)

    size = lax.axis_size("slab")
    up = [(i, i + 1) for i in range(size - 1)]
    down = [(i + 1, i) for i in range(size - 1)]
    rows = query.shape[0]
    edge = FACE * BLOCK // rows
    half, chunk = rows // 2, rows // CHUNKS
    one, two = pack_heads(key, value, query, grad_out)
    one = exchange(one)
    first, last = take_faces(one, edge, rows)
    before = lax.ppermute(last, "slab", up)
    after = lax.ppermute(first, "slab", down)
    two = exchange(two)
    start = (lax.axis_index("slab") * pattern.shape[0] - FACE).astype(jnp.int32).reshape(1)
    scalars = (pattern.reshape(-1), valid_rows, start)
    od, kv, acc = first_half(*scalars, one, before, after)
    od = exchange(od)
    z, first, last, to_before, to_after = second_half(*scalars, two, kv, acc, edge)
    high = lax.ppermute(to_before, "slab", down)
    low = lax.ppermute(to_after, "slab", up)
    done = unpack_heads(od, rows, chunks(0, 0, half, 0, chunk), 2, "unpack_first")
    z, *done = lax.optimization_barrier((z, *done))
    z = exchange(join_faces(z, first, last, low, high))
    jobs = chunks(0, 0, rows, 0, chunk) + chunks(2, half, half, rows, chunk)
    grad_key, grad_value, grad_query, attn_out = unpack_heads(
        z, rows, jobs, 4, "unpack_second", into=done
    )
    return (attn_out, grad_query, grad_key, grad_value)


def solution(mesh):
    rows = P(("slab", "seq"), None)
    return jax.shard_map(
        body,
        mesh=mesh,
        in_specs=(rows, rows, rows, rows, P("slab", None), P()),
        out_specs=(rows, rows, rows, rows),
        check_vma=False,
    )
```

```python
from functools import partial
import math

import jax
import jax.numpy as jnp
from jax import lax
from jax.experimental import pallas as pl
from jax.experimental.pallas import tpu as pltpu
from jax.sharding import PartitionSpec as P

HEAD_DIM = 64
BLOCK = 64
FACE = 16
PAIR = 2 * HEAD_DIM
CHUNKS = 4

score_scale = 0.125
exp2_scale = score_scale * math.log2(math.e)


def on_chip(x):
    return pltpu.with_memory_space_constraint(x, pltpu.VMEM)


def off_chip(x):
    return pltpu.with_memory_space_constraint(x, pltpu.HBM)


def faces_kernel(odd_ref, x_hbm, inner_ref, outer_ref, sems):
    edge, rows = inner_ref.shape[:2]
    end = x_hbm.shape[0] - edge
    odd = odd_ref[0]
    copies = [
        pltpu.make_async_copy(x_hbm.at[pl.ds(at, edge), pl.ds(0, rows)], ref, sems.at[i])
        for i, (at, ref) in enumerate((((1 - odd) * end, inner_ref), (odd * end, outer_ref)))
    ]
    for copy in copies:
        copy.start()
    for copy in copies:
        copy.wait()


def take_faces(odd, x, edge, rows):
    vmem = pl.BlockSpec(memory_space=pltpu.VMEM)
    return pl.pallas_call(
        faces_kernel,
        out_shape=(pltpu.VMEM((edge, rows, PAIR), x.dtype),) * 2,
        in_specs=[pl.BlockSpec(memory_space=pltpu.SMEM), pl.BlockSpec(memory_space=pltpu.HBM)],
        out_specs=(vmem, vmem),
        scratch_shapes=[pltpu.SemaphoreType.DMA((2,))],
        compiler_params=pltpu.CompilerParams(vmem_limit_bytes=4 << 20),
        name="take_faces",
    )(odd, off_chip(x))


def swap_halves(a, b):
    low = jnp.concatenate([a[:, :HEAD_DIM], b[:, :HEAD_DIM]], axis=1)
    high = jnp.concatenate([a[:, HEAD_DIM:], b[:, HEAD_DIM:]], axis=1)
    return low, high


def pack_kernel(
    k_hbm, v_hbm, q_hbm, g_hbm, one_hbm, two_hbm, in_refs, out_refs, in_sems, one_sems, two_sems,
):
    rows, half = k_hbm.shape[0], two_hbm.shape[1]
    chunk = rows // CHUNKS
    pairs = ((k_hbm, v_hbm), (q_hbm, g_hbm))

    def span(c):
        return pl.ds(c * chunk, chunk)

    def load(n, i, c):
        return pltpu.make_async_copy(
            pairs[n][i].at[span(c)], in_refs.at[2 * n + i, span(c)], in_sems.at[2 * n + i, c]
        )

    def store(n, c):
        if n == 0 or c * chunk < half:
            target = one_hbm.at[:, pl.ds(n * rows + c * chunk, chunk)]
        else:
            target = two_hbm.at[:, pl.ds(c * chunk - half, chunk)]
        return pltpu.make_async_copy(
            out_refs.at[n, :, span(c)], target, (one_sems if n == 0 else two_sems).at[c]
        )

    order = [(n, c) for n in range(2) for c in range(CHUNKS)]
    for n, c in order:
        for i in range(2):
            load(n, i, c).start()
    for n, c in order:
        for i in range(2):
            load(n, i, c).wait()
        part = slice(c * chunk, (c + 1) * chunk)
        for p in range(k_hbm.shape[1] // PAIR):
            cols = slice(p * PAIR, (p + 1) * PAIR)
            halves = swap_halves(in_refs[2 * n, part, cols], in_refs[2 * n + 1, part, cols])
            out_refs[n, 2 * p, part], out_refs[n, 2 * p + 1, part] = halves
        store(n, c).start()
    for n, c in order:
        store(n, c).wait()


def pack_heads(k, v, q, g):
    rows, cols = k.shape
    heads, half = cols // HEAD_DIM, rows // 2
    hbm = pl.BlockSpec(memory_space=pltpu.HBM)
    return pl.pallas_call(
        pack_kernel,
        out_shape=tuple(pltpu.HBM((heads, size, PAIR), k.dtype) for size in (rows + half, half)),
        in_specs=[hbm] * 4,
        out_specs=(hbm, hbm),
        scratch_shapes=[
            pltpu.VMEM((4, rows, cols), k.dtype),
            pltpu.VMEM((2, heads, rows, PAIR), k.dtype),
            pltpu.SemaphoreType.DMA((4, CHUNKS)),
            pltpu.SemaphoreType.DMA((CHUNKS,)),
            pltpu.SemaphoreType.DMA((CHUNKS,)),
        ],
        compiler_params=pltpu.CompilerParams(vmem_limit_bytes=60 << 20),
        name="pack_heads",
    )(*(off_chip(x) for x in (k, v, q, g)))


def chunks(source, row, size, to, chunk):
    return [(source, row + i, chunk, to + i) for i in range(0, size, chunk)]


def unpack_kernel(*refs, jobs, count, skip):
    source, targets = refs[0], refs[1 + skip : 1 + skip + count]
    out_refs, sems = refs[1 + skip + count :]

    def store(n, i):
        target, row, size, at = jobs[n]
        return pltpu.make_async_copy(
            out_refs.at[i, pl.ds(at, size)], targets[target + i].at[pl.ds(row, size)], sems.at[i, n]
        )

    for n, (_, _, size, at) in enumerate(jobs):
        part = slice(at, at + size)
        for p in range(source.shape[0] // 2):
            cols = slice(p * PAIR, (p + 1) * PAIR)
            halves = swap_halves(source[2 * p, part], source[2 * p + 1, part])
            out_refs[0, part, cols], out_refs[1, part, cols] = halves
        for i in range(2):
            store(n, i).start()
    for n in range(len(jobs)):
        for i in range(2):
            store(n, i).wait()


def unpack_heads(x, full_rows, jobs, count, name, into=()):
    heads, rows, _ = x.shape
    cols = heads * HEAD_DIM
    hbm = pl.BlockSpec(memory_space=pltpu.HBM)
    return pl.pallas_call(
        partial(unpack_kernel, jobs=jobs, count=count, skip=len(into)),
        out_shape=(pltpu.HBM((full_rows, cols), x.dtype),) * count,
        in_specs=[pl.BlockSpec(memory_space=pltpu.VMEM)] + [hbm] * len(into),
        out_specs=(hbm,) * count,
        scratch_shapes=[
            pltpu.VMEM((2, rows, cols), x.dtype),
            pltpu.SemaphoreType.DMA((2, len(jobs))),
        ],
        input_output_aliases={1 + i: count - len(into) + i for i in range(len(into))},
        compiler_params=pltpu.CompilerParams(vmem_limit_bytes=16 << 20),
        cost_estimate=pl.CostEstimate(
            flops=0, transcendentals=0, bytes_accessed=4 * rows * cols * x.dtype.itemsize
        ),
        name=name,
    )(on_chip(x), *(off_chip(a) for a in into))


def in_turn(*tasks):
    def steps(stage, blocks):
        for u in blocks:
            yield from stage(u)

    running = [steps(*task) for task in tasks]
    while running:
        running = [task for task in running if next(task, True) is None]


def query_blocks(
    pattern_ref, valid_ref, start_ref, kv_ref, qg_ref, acc_ref, od_ref, both_ref, pd_ref, send_od,
    *, keys_num, chunk, group, lines, ready=None,
):
    shards, rows = qg_ref.shape[:2]
    each = rows // BLOCK
    start = start_ref[0]
    low = lax.broadcasted_iota(jnp.int32, (BLOCK, PAIR), 1) < HEAD_DIM
    lane = lax.broadcasted_iota(jnp.int32, (1, PAIR), 1)

    def one_group(t, _):
        shard = t * (group // each)
        meta = []
        for u in range(group):
            s, i = u // each, u % each
            base = ((shard + s) * 2 * each + chunk * each + i) * keys_num
            slots = [pattern_ref[base + j] for j in range(keys_num)]
            counts = [valid_ref[start + slot] for slot in slots]
            meta.append((s, slice(i * BLOCK, (i + 1) * BLOCK), slots, counts))

        def gathered(slots):
            return jnp.concatenate(
                [kv_ref[pl.ds(pl.multiple_of(slot * BLOCK, BLOCK), BLOCK), :] for slot in slots],
                axis=0,
            )

        def spread(s, part):
            qg = qg_ref[shard + s, part, :]
            zero = jnp.zeros_like(qg)
            return jnp.concatenate([jnp.where(low, zero, qg), jnp.where(low, qg, zero)], axis=0)

        def probe(u):
            s, part, slots, counts = meta[u]
            kv, gq = gathered(slots), spread(s, part)
            for n in range(0, keys_num * BLOCK, 2 * PAIR):
                both_ref[u, :, n : n + 2 * PAIR] = lax.dot_general(
                    gq, kv[n : n + 2 * PAIR], (((1,), (1,)), ((), ())),
                    preferred_element_type=jnp.float32,
                )
                yield

        def weigh(u):
            s, part, slots, counts = meta[u]
            bias = jnp.concatenate(
                [
                    jnp.where(
                        lane < jnp.where(lane < HEAD_DIM, counts[j], counts[j + 1] + HEAD_DIM),
                        0.0,
                        -jnp.inf,
                    )
                    for j in range(0, keys_num, 2)
                ],
                axis=1,
            )
            for r in range(0, BLOCK, lines):
                scores = both_ref[u, BLOCK + r : BLOCK + r + lines, :] + bias
                top = jnp.max(scores, axis=1, keepdims=True)
                weight = jnp.exp2((scores - top) * exp2_scale)
                total = jnp.sum(weight, axis=1, keepdims=True)
                prob = (weight * (1.0 / total)).astype(jnp.bfloat16)
                prob_wide = prob.astype(jnp.float32)
                grad_prob = both_ref[u, r : r + lines, :]
                delta = jnp.sum(prob_wide * grad_prob, axis=1, keepdims=True)
                dscore = (prob_wide * (grad_prob - delta)).astype(jnp.bfloat16)
                pd_ref[u, r : r + lines, :] = prob
                pd_ref[u, BLOCK + r : BLOCK + r + lines, :] = dscore
                yield

        def rows_out(u):
            s, part, slots, counts = meta[u]
            od = jnp.dot(pd_ref[u], gathered(slots), preferred_element_type=jnp.float32)
            od_ref[shard + s, part, :] = jnp.where(
                low, od[BLOCK:] * score_scale, od[:BLOCK]
            ).astype(od_ref.dtype)
            yield

        def keys_out(u):
            s, part, slots, counts = meta[u]
            dkv = lax.dot_general(
                pd_ref[u], spread(s, part), (((0,), (0,)), ((), ())),
                preferred_element_type=jnp.float32,
            )
            yield
            for j, slot in enumerate(slots):
                span = pl.ds(pl.multiple_of(slot * BLOCK, BLOCK), BLOCK)
                acc_ref[span, :] += dkv[j * BLOCK : (j + 1) * BLOCK]
                if j % 2:
                    yield

        near, far = range(group // 2), range(group // 2, group)
        in_turn((probe, near))
        in_turn((probe, far), (weigh, near))
        if ready is not None:
            pl.when(t == 0)(ready)
        in_turn((keys_out, near), (weigh, far))
        in_turn((rows_out, range(group)))
        for s in range(group // each):
            send_od(shard + s).start()
        in_turn((keys_out, far))
        return 0

    lax.fori_loop(0, shards * each // group, one_group, 0)


def first_kernel(
    pattern_ref, valid_ref, start_ref, odd_ref, x_hbm, inner_ref, outer_ref,
    od_hbm, kv_hbm, acc_hbm,
    kv_ref, acc_ref, qg_ref, od_ref, both_ref, pd_ref, in_sems, od_sems, out_sems, **sizes,
):
    shards, half = qg_ref.shape[:2]
    rows = x_hbm.shape[1] - half
    edge = inner_ref.shape[0]
    above = edge + shards
    odd = odd_ref[0]

    def fetch(source, at, i):
        span = pl.ds(pl.multiple_of(at * rows, rows), rows)
        return pltpu.make_async_copy(source, kv_ref.at[span], in_sems.at[i])

    copies = [fetch(x_hbm.at[t, pl.ds(0, rows)], edge + t, t) for t in range(shards)]
    for t in range(edge):
        copies += [fetch(inner_ref.at[t], (1 - odd) * above + t, len(copies))]
        copies += [fetch(outer_ref.at[t], odd * above + t, len(copies))]
    copies += [
        pltpu.make_async_copy(x_hbm.at[:, pl.ds(rows, half)], qg_ref, in_sems.at[len(copies)])
    ]
    for copy in copies:
        copy.start()
    acc_ref[...] = jnp.zeros_like(acc_ref)
    for copy in copies:
        copy.wait()
    keep = pltpu.make_async_copy(kv_ref, kv_hbm, out_sems.at[0])
    keep.start()

    def send_od(t):
        return pltpu.make_async_copy(od_ref.at[t], od_hbm.at[t], od_sems.at[t])

    query_blocks(
        pattern_ref, valid_ref, start_ref, kv_ref, qg_ref, acc_ref, od_ref, both_ref, pd_ref,
        send_od, chunk=0, **sizes,
    )
    total = pltpu.make_async_copy(acc_ref, acc_hbm, out_sems.at[1])
    total.start()
    for t in range(shards):
        send_od(t).wait()
    keep.wait()
    total.wait()


def second_kernel(
    pattern_ref, valid_ref, start_ref, odd_ref, qg_ref, kv_hbm, acc_hbm,
    z_hbm, inner_own_ref, outer_own_ref, inner_rim_ref, outer_rim_ref,
    kv_ref, acc_ref, od_ref, dkv_ref, both_ref, pd_ref, in_sems, od_sems, dkv_sems, **sizes,
):
    shards, half = qg_ref.shape[:2]
    rows = 2 * half
    edge = inner_own_ref.shape[0]
    copies = [
        pltpu.make_async_copy(source, target, in_sems.at[i])
        for i, (source, target) in enumerate(((kv_hbm, kv_ref), (acc_hbm, acc_ref)))
    ]
    for copy in copies:
        copy.start()
    copies[0].wait()

    def send_od(t):
        return pltpu.make_async_copy(od_ref.at[t], z_hbm.at[t, pl.ds(rows, half)], od_sems.at[t])

    def send_dkv(t):
        return pltpu.make_async_copy(dkv_ref.at[t], z_hbm.at[t, pl.ds(0, rows)], dkv_sems.at[t])

    query_blocks(
        pattern_ref, valid_ref, start_ref, kv_ref, qg_ref, acc_ref, od_ref, both_ref, pd_ref,
        send_od, chunk=1, ready=copies[1].wait, **sizes,
    )
    low = lax.broadcasted_iota(jnp.int32, (rows, PAIR), 1) < HEAD_DIM

    def scaled(s):
        tile = acc_ref[pl.ds(pl.multiple_of(s * rows, rows), rows), :]
        return jnp.where(low, tile * score_scale, tile)

    for t in range(edge, shards - edge):
        dkv_ref[t] = scaled(edge + t).astype(dkv_ref.dtype)
        send_dkv(t).start()
    odd, above, end = odd_ref[0], edge + shards, shards - edge
    for s in range(edge):
        inner_rim_ref[s] = scaled((1 - odd) * above + s).astype(inner_rim_ref.dtype)
        outer_rim_ref[s] = scaled(odd * above + s).astype(outer_rim_ref.dtype)
        inner_own_ref[s] = scaled(edge + (1 - odd) * end + s)
        outer_own_ref[s] = scaled(edge + odd * end + s)
    for t in range(shards):
        send_od(t).wait()
    for t in range(edge, shards - edge):
        send_dkv(t).wait()


def cost(tokens, keys_num):
    work = tokens * keys_num * BLOCK
    return pl.CostEstimate(flops=12 * PAIR * work, transcendentals=work, bytes_accessed=16 << 20)


def first_half(pattern, valid_rows, start, odd, x, inner, outer, group=16, lines=16):
    keys_num = pattern.shape[0] * BLOCK // (x.shape[0] * inner.shape[1])
    shards, edge, rows = x.shape[0], inner.shape[0], inner.shape[1]
    half, ext = rows // 2, shards + 2 * edge
    smem = pl.BlockSpec(memory_space=pltpu.SMEM)
    hbm = pl.BlockSpec(memory_space=pltpu.HBM)
    vmem = pl.BlockSpec(memory_space=pltpu.VMEM)
    return pl.pallas_call(
        partial(first_kernel, keys_num=keys_num, group=group, lines=lines),
        out_shape=(
            pltpu.HBM((shards, half, PAIR), x.dtype),
            pltpu.HBM((ext * rows, PAIR), x.dtype),
            pltpu.HBM((ext * rows, PAIR), jnp.float32),
        ),
        in_specs=[smem, smem, smem, smem, hbm, vmem, vmem],
        out_specs=(hbm, hbm, hbm),
        scratch_shapes=[
            pltpu.VMEM((ext * rows, PAIR), x.dtype),
            pltpu.VMEM((ext * rows, PAIR), jnp.float32),
            pltpu.VMEM((shards, half, PAIR), x.dtype),
            pltpu.VMEM((shards, half, PAIR), x.dtype),
            pltpu.VMEM((group, PAIR, keys_num * BLOCK), jnp.float32),
            pltpu.VMEM((group, PAIR, keys_num * BLOCK), x.dtype),
            pltpu.SemaphoreType.DMA((ext + 1,)),
            pltpu.SemaphoreType.DMA((shards,)),
            pltpu.SemaphoreType.DMA((2,)),
        ],
        compiler_params=pltpu.CompilerParams(vmem_limit_bytes=32 << 20),
        cost_estimate=cost(shards * half, keys_num),
        name="first_half",
    )(pattern, valid_rows, start, odd, off_chip(x), on_chip(inner), on_chip(outer))


def second_half(pattern, valid_rows, start, odd, x, kv, acc, edge, group=32, lines=16):
    shards, half = x.shape[:2]
    rows = 2 * half
    keys_num = pattern.shape[0] * BLOCK // (shards * rows)
    smem = pl.BlockSpec(memory_space=pltpu.SMEM)
    hbm = pl.BlockSpec(memory_space=pltpu.HBM)
    vmem = pl.BlockSpec(memory_space=pltpu.VMEM)
    face = (edge, rows, PAIR)
    return pl.pallas_call(
        partial(second_kernel, keys_num=keys_num, group=group, lines=lines),
        out_shape=(pltpu.HBM((shards, rows + half, PAIR), x.dtype),)
        + (pltpu.VMEM(face, jnp.float32),) * 2
        + (pltpu.VMEM(face, x.dtype),) * 2,
        in_specs=[smem, smem, smem, smem, vmem, hbm, hbm],
        out_specs=(hbm, vmem, vmem, vmem, vmem),
        scratch_shapes=[
            pltpu.VMEM(kv.shape, kv.dtype),
            pltpu.VMEM(acc.shape, acc.dtype),
            pltpu.VMEM((shards, half, PAIR), x.dtype),
            pltpu.VMEM((shards, rows, PAIR), x.dtype),
            pltpu.VMEM((group, PAIR, keys_num * BLOCK), jnp.float32),
            pltpu.VMEM((group, PAIR, keys_num * BLOCK), x.dtype),
            pltpu.SemaphoreType.DMA((2,)),
            pltpu.SemaphoreType.DMA((shards,)),
            pltpu.SemaphoreType.DMA((shards,)),
        ],
        compiler_params=pltpu.CompilerParams(vmem_limit_bytes=32 << 20),
        cost_estimate=cost(shards * half, keys_num),
        name="second_half",
    )(pattern, valid_rows, start, odd, on_chip(x), off_chip(kv), off_chip(acc))


def join_kernel(
    odd_ref, z_in, inner_ref, outer_ref, inner_rim_ref, outer_rim_ref, z_hbm, sum_ref, sems,
):
    edge, rows = inner_ref.shape[:2]
    odd = odd_ref[0]
    shards = z_hbm.shape[0]
    sum_ref[0] = (inner_ref[...] + inner_rim_ref[...].astype(jnp.float32)).astype(sum_ref.dtype)
    sum_ref[1] = (outer_ref[...] + outer_rim_ref[...].astype(jnp.float32)).astype(sum_ref.dtype)
    copies = [
        pltpu.make_async_copy(
            sum_ref.at[i], z_hbm.at[pl.ds(at, edge), pl.ds(0, rows)], sems.at[i]
        )
        for i, at in enumerate(((1 - odd) * (shards - edge), odd * (shards - edge)))
    ]
    for copy in copies:
        copy.start()
    for copy in copies:
        copy.wait()


def join_faces(odd, z, inner, outer, inner_rim, outer_rim):
    hbm = pl.BlockSpec(memory_space=pltpu.HBM)
    vmem = pl.BlockSpec(memory_space=pltpu.VMEM)
    return pl.pallas_call(
        join_kernel,
        out_shape=pltpu.HBM(z.shape, z.dtype),
        in_specs=[pl.BlockSpec(memory_space=pltpu.SMEM), hbm, vmem, vmem, vmem, vmem],
        out_specs=hbm,
        scratch_shapes=[pltpu.VMEM((2, *inner_rim.shape), z.dtype), pltpu.SemaphoreType.DMA((2,))],
        input_output_aliases={1: 0},
        compiler_params=pltpu.CompilerParams(vmem_limit_bytes=8 << 20),
        name="join_faces",
    )(odd, z, *(on_chip(a) for a in (inner, outer, inner_rim, outer_rim)))


def body(query, key, value, grad_out, pattern, valid_rows):
    def exchange(x):
        return lax.all_to_all(x, "seq", split_axis=0, concat_axis=0, tiled=True)

    size = lax.axis_size("slab")
    inside = [(i, i ^ 1) for i in range(size) if i ^ 1 < size]
    outside = [(i, j) for i in range(size) if 0 <= (j := i - 1 + 2 * (i % 2)) < size]
    odd = (lax.axis_index("slab") % 2).astype(jnp.int32).reshape(1)
    rows = query.shape[0]
    edge = FACE * BLOCK // rows
    half, chunk = rows // 2, rows // CHUNKS
    one, two = pack_heads(key, value, query, grad_out)
    one = exchange(one)
    inner, outer = take_faces(odd, one, edge, rows)
    inner = lax.ppermute(inner, "slab", inside)
    outer = lax.ppermute(outer, "slab", outside)
    two = exchange(two)
    start = (lax.axis_index("slab") * pattern.shape[0] - FACE).astype(jnp.int32).reshape(1)
    scalars = (pattern.reshape(-1), valid_rows, start, odd)
    od, kv, acc = first_half(*scalars, one, inner, outer)
    od = exchange(od)
    z, inner, outer, inner_rim, outer_rim = second_half(*scalars, two, kv, acc, edge)
    inner_rim = lax.ppermute(inner_rim, "slab", inside)
    outer_rim = lax.ppermute(outer_rim, "slab", outside)
    done = unpack_heads(od, rows, chunks(0, 0, half, 0, chunk), 2, "unpack_first")
    z, *done = lax.optimization_barrier((z, *done))
    z = exchange(join_faces(odd, z, inner, outer, inner_rim, outer_rim))
    jobs = chunks(0, 0, rows, 0, chunk) + chunks(2, half, half, rows, chunk)
    grad_key, grad_value, grad_query, attn_out = unpack_heads(
        z, rows, jobs, 4, "unpack_second", into=done
    )
    return (attn_out, grad_query, grad_key, grad_value)


def solution(mesh):
    rows = P(("slab", "seq"), None)
    return jax.shard_map(
        body,
        mesh=mesh,
        in_specs=(rows, rows, rows, rows, P("slab", None), P()),
        out_specs=(rows, rows, rows, rows),
        check_vma=False,
    )
```

```python
from functools import partial
import math

import jax
import jax.numpy as jnp
from jax import lax
from jax.experimental import pallas as pl
from jax.experimental.pallas import tpu as pltpu
from jax.sharding import PartitionSpec as P

HEAD_DIM = 64
BLOCK = 64
FACE = 16
PAIR = 2 * HEAD_DIM
CHUNKS = 4

score_scale = 0.125
exp2_scale = score_scale * math.log2(math.e)


def on_chip(x):
    return pltpu.with_memory_space_constraint(x, pltpu.VMEM)


def off_chip(x):
    return pltpu.with_memory_space_constraint(x, pltpu.HBM)


def faces_kernel(odd_ref, x_hbm, inner_ref, outer_ref, sems):
    edge, rows = inner_ref.shape[:2]
    end = x_hbm.shape[0] - edge
    odd = odd_ref[0]
    copies = [
        pltpu.make_async_copy(x_hbm.at[pl.ds(at, edge), pl.ds(0, rows)], ref, sems.at[i])
        for i, (at, ref) in enumerate((((1 - odd) * end, inner_ref), (odd * end, outer_ref)))
    ]
    for copy in copies:
        copy.start()
    for copy in copies:
        copy.wait()


def take_faces(odd, x, edge, rows):
    vmem = pl.BlockSpec(memory_space=pltpu.VMEM)
    return pl.pallas_call(
        faces_kernel,
        out_shape=(pltpu.VMEM((edge, rows, PAIR), x.dtype),) * 2,
        in_specs=[pl.BlockSpec(memory_space=pltpu.SMEM), pl.BlockSpec(memory_space=pltpu.HBM)],
        out_specs=(vmem, vmem),
        scratch_shapes=[pltpu.SemaphoreType.DMA((2,))],
        compiler_params=pltpu.CompilerParams(vmem_limit_bytes=4 << 20),
        name="take_faces",
    )(odd, off_chip(x))


def swap_halves(a, b):
    low = jnp.concatenate([a[:, :HEAD_DIM], b[:, :HEAD_DIM]], axis=1)
    high = jnp.concatenate([a[:, HEAD_DIM:], b[:, HEAD_DIM:]], axis=1)
    return low, high


def pack_kernel(
    k_hbm, v_hbm, q_hbm, g_hbm, one_hbm, two_hbm, in_refs, out_refs, in_sems, one_sems, two_sems,
):
    rows, half = k_hbm.shape[0], two_hbm.shape[1]
    chunk = rows // CHUNKS
    pairs = ((k_hbm, v_hbm), (q_hbm, g_hbm))

    def span(c):
        return pl.ds(c * chunk, chunk)

    def load(n, i, c):
        return pltpu.make_async_copy(
            pairs[n][i].at[span(c)], in_refs.at[2 * n + i, span(c)], in_sems.at[2 * n + i, c]
        )

    def store(n, c):
        if n == 0 or c * chunk < half:
            target = one_hbm.at[:, pl.ds(n * rows + c * chunk, chunk)]
        else:
            target = two_hbm.at[:, pl.ds(c * chunk - half, chunk)]
        return pltpu.make_async_copy(
            out_refs.at[n, :, span(c)], target, (one_sems if n == 0 else two_sems).at[c]
        )

    order = [(n, c) for n in range(2) for c in range(CHUNKS)]
    for n, c in order:
        for i in range(2):
            load(n, i, c).start()
    for n, c in order:
        for i in range(2):
            load(n, i, c).wait()
        part = slice(c * chunk, (c + 1) * chunk)
        for p in range(k_hbm.shape[1] // PAIR):
            cols = slice(p * PAIR, (p + 1) * PAIR)
            halves = swap_halves(in_refs[2 * n, part, cols], in_refs[2 * n + 1, part, cols])
            out_refs[n, 2 * p, part], out_refs[n, 2 * p + 1, part] = halves
        store(n, c).start()
    for n, c in order:
        store(n, c).wait()


def pack_heads(k, v, q, g):
    rows, cols = k.shape
    heads, half = cols // HEAD_DIM, rows // 2
    hbm = pl.BlockSpec(memory_space=pltpu.HBM)
    return pl.pallas_call(
        pack_kernel,
        out_shape=tuple(pltpu.HBM((heads, size, PAIR), k.dtype) for size in (rows + half, half)),
        in_specs=[hbm] * 4,
        out_specs=(hbm, hbm),
        scratch_shapes=[
            pltpu.VMEM((4, rows, cols), k.dtype),
            pltpu.VMEM((2, heads, rows, PAIR), k.dtype),
            pltpu.SemaphoreType.DMA((4, CHUNKS)),
            pltpu.SemaphoreType.DMA((CHUNKS,)),
            pltpu.SemaphoreType.DMA((CHUNKS,)),
        ],
        compiler_params=pltpu.CompilerParams(vmem_limit_bytes=60 << 20),
        name="pack_heads",
    )(*(off_chip(x) for x in (k, v, q, g)))


def chunks(source, row, size, to, chunk):
    return [(source, row + i, chunk, to + i) for i in range(0, size, chunk)]


def unpack_kernel(*refs, jobs, count, skip):
    source, targets = refs[0], refs[1 + skip : 1 + skip + count]
    out_refs, sems = refs[1 + skip + count :]

    def store(n, i):
        target, row, size, at = jobs[n]
        return pltpu.make_async_copy(
            out_refs.at[i, pl.ds(at, size)], targets[target + i].at[pl.ds(row, size)], sems.at[i, n]
        )

    for n, (_, _, size, at) in enumerate(jobs):
        part = slice(at, at + size)
        for p in range(source.shape[0] // 2):
            cols = slice(p * PAIR, (p + 1) * PAIR)
            halves = swap_halves(source[2 * p, part], source[2 * p + 1, part])
            out_refs[0, part, cols], out_refs[1, part, cols] = halves
        for i in range(2):
            store(n, i).start()
    for n in range(len(jobs)):
        for i in range(2):
            store(n, i).wait()


def unpack_heads(x, full_rows, jobs, count, name, into=()):
    heads, rows, _ = x.shape
    cols = heads * HEAD_DIM
    hbm = pl.BlockSpec(memory_space=pltpu.HBM)
    return pl.pallas_call(
        partial(unpack_kernel, jobs=jobs, count=count, skip=len(into)),
        out_shape=(pltpu.HBM((full_rows, cols), x.dtype),) * count,
        in_specs=[pl.BlockSpec(memory_space=pltpu.VMEM)] + [hbm] * len(into),
        out_specs=(hbm,) * count,
        scratch_shapes=[
            pltpu.VMEM((2, rows, cols), x.dtype),
            pltpu.SemaphoreType.DMA((2, len(jobs))),
        ],
        input_output_aliases={1 + i: count - len(into) + i for i in range(len(into))},
        compiler_params=pltpu.CompilerParams(vmem_limit_bytes=16 << 20),
        cost_estimate=pl.CostEstimate(
            flops=0, transcendentals=0, bytes_accessed=4 * rows * cols * x.dtype.itemsize
        ),
        name=name,
    )(on_chip(x), *(off_chip(a) for a in into))


def in_turn(*tasks):
    def steps(stage, blocks):
        for u in blocks:
            yield from stage(u)

    running = [steps(*task) for task in tasks]
    while running:
        running = [task for task in running if next(task, True) is None]


def query_blocks(
    pattern_ref, valid_ref, start_ref, kv_ref, qg_ref, acc_ref, od_ref, both_ref, pd_ref, send_od,
    *, keys_num, chunk, group, lines, ready=None,
):
    shards, rows = qg_ref.shape[:2]
    each = rows // BLOCK
    start = start_ref[0]
    low = lax.broadcasted_iota(jnp.int32, (BLOCK, PAIR), 1) < HEAD_DIM
    lane = lax.broadcasted_iota(jnp.int32, (1, PAIR), 1)

    def one_group(t, _):
        shard = t * (group // each)
        meta = []
        for u in range(group):
            s, i = u // each, u % each
            base = ((shard + s) * 2 * each + chunk * each + i) * keys_num
            slots = [pattern_ref[base + j] for j in range(keys_num)]
            counts = [valid_ref[start + slot] for slot in slots]
            meta.append((s, slice(i * BLOCK, (i + 1) * BLOCK), slots, counts))

        def gathered(slots):
            return jnp.concatenate(
                [kv_ref[pl.ds(pl.multiple_of(slot * BLOCK, BLOCK), BLOCK), :] for slot in slots],
                axis=0,
            )

        def spread(s, part):
            qg = qg_ref[shard + s, part, :]
            zero = jnp.zeros_like(qg)
            return jnp.concatenate([jnp.where(low, zero, qg), jnp.where(low, qg, zero)], axis=0)

        def probe(u):
            s, part, slots, counts = meta[u]
            kv, gq = gathered(slots), spread(s, part)
            for n in range(0, keys_num * BLOCK, 2 * PAIR):
                both_ref[u, :, n : n + 2 * PAIR] = lax.dot_general(
                    gq, kv[n : n + 2 * PAIR], (((1,), (1,)), ((), ())),
                    preferred_element_type=jnp.float32,
                )
                yield

        def weigh(u):
            s, part, slots, counts = meta[u]
            bias = jnp.concatenate(
                [
                    jnp.where(
                        lane < jnp.where(lane < HEAD_DIM, counts[j], counts[j + 1] + HEAD_DIM),
                        0.0,
                        -jnp.inf,
                    )
                    for j in range(0, keys_num, 2)
                ],
                axis=1,
            )
            for r in range(0, BLOCK, lines):
                scores = both_ref[u, BLOCK + r : BLOCK + r + lines, :] + bias
                top = jnp.max(scores, axis=1, keepdims=True)
                weight = jnp.exp2((scores - top) * exp2_scale)
                total = jnp.sum(weight, axis=1, keepdims=True)
                prob = (weight * (1.0 / total)).astype(jnp.bfloat16)
                prob_wide = prob.astype(jnp.float32)
                grad_prob = both_ref[u, r : r + lines, :]
                delta = jnp.sum(prob_wide * grad_prob, axis=1, keepdims=True)
                dscore = (prob_wide * (grad_prob - delta)).astype(jnp.bfloat16)
                pd_ref[u, r : r + lines, :] = prob
                pd_ref[u, BLOCK + r : BLOCK + r + lines, :] = dscore
                yield

        def rows_out(u):
            s, part, slots, counts = meta[u]
            od = jnp.dot(pd_ref[u], gathered(slots), preferred_element_type=jnp.float32)
            od_ref[shard + s, part, :] = jnp.where(
                low, od[BLOCK:] * score_scale, od[:BLOCK]
            ).astype(od_ref.dtype)
            yield

        def keys_out(u):
            s, part, slots, counts = meta[u]
            dkv = lax.dot_general(
                pd_ref[u], spread(s, part), (((0,), (0,)), ((), ())),
                preferred_element_type=jnp.float32,
            )
            yield
            for j, slot in enumerate(slots):
                span = pl.ds(pl.multiple_of(slot * BLOCK, BLOCK), BLOCK)
                acc_ref[span, :] += dkv[j * BLOCK : (j + 1) * BLOCK]
                if j % 2:
                    yield

        near, far = range(group // 2), range(group // 2, group)
        in_turn((probe, near))
        in_turn((probe, far), (weigh, near))
        if ready is not None:
            pl.when(t == 0)(ready)
        in_turn((keys_out, near), (weigh, far))
        in_turn((rows_out, range(group)))
        for s in range(group // each):
            send_od(shard + s).start()
        in_turn((keys_out, far))
        return 0

    lax.fori_loop(0, shards * each // group, one_group, 0)


def first_kernel(
    pattern_ref, valid_ref, start_ref, odd_ref, x_hbm, inner_ref, outer_ref,
    od_hbm, kv_hbm, acc_hbm,
    kv_ref, acc_ref, qg_ref, od_ref, both_ref, pd_ref, in_sems, od_sems, out_sems, **sizes,
):
    shards, half = qg_ref.shape[:2]
    rows = x_hbm.shape[1] - half
    edge = inner_ref.shape[0]
    above = edge + shards
    odd = odd_ref[0]

    def fetch(source, at, i):
        span = pl.ds(pl.multiple_of(at * rows, rows), rows)
        return pltpu.make_async_copy(source, kv_ref.at[span], in_sems.at[i])

    copies = [fetch(x_hbm.at[t, pl.ds(0, rows)], edge + t, t) for t in range(shards)]
    for t in range(edge):
        copies += [fetch(inner_ref.at[t], (1 - odd) * above + t, len(copies))]
        copies += [fetch(outer_ref.at[t], odd * above + t, len(copies))]
    copies += [
        pltpu.make_async_copy(x_hbm.at[:, pl.ds(rows, half)], qg_ref, in_sems.at[len(copies)])
    ]
    for copy in copies:
        copy.start()
    acc_ref[...] = jnp.zeros_like(acc_ref)
    for copy in copies:
        copy.wait()
    keep = pltpu.make_async_copy(kv_ref, kv_hbm, out_sems.at[0])
    keep.start()

    def send_od(t):
        return pltpu.make_async_copy(od_ref.at[t], od_hbm.at[t], od_sems.at[t])

    query_blocks(
        pattern_ref, valid_ref, start_ref, kv_ref, qg_ref, acc_ref, od_ref, both_ref, pd_ref,
        send_od, chunk=0, **sizes,
    )
    total = pltpu.make_async_copy(acc_ref, acc_hbm, out_sems.at[1])
    total.start()
    for t in range(shards):
        send_od(t).wait()
    keep.wait()
    total.wait()


def second_kernel(
    pattern_ref, valid_ref, start_ref, odd_ref, qg_ref, kv_hbm, acc_hbm,
    z_hbm, inner_own_ref, outer_own_ref, inner_rim_ref, outer_rim_ref,
    kv_ref, acc_ref, od_ref, dkv_ref, both_ref, pd_ref, in_sems, od_sems, dkv_sems, **sizes,
):
    shards, half = qg_ref.shape[:2]
    rows = 2 * half
    edge = inner_own_ref.shape[0]
    copies = [
        pltpu.make_async_copy(source, target, in_sems.at[i])
        for i, (source, target) in enumerate(((kv_hbm, kv_ref), (acc_hbm, acc_ref)))
    ]
    for copy in copies:
        copy.start()
    copies[0].wait()

    def send_od(t):
        return pltpu.make_async_copy(od_ref.at[t], z_hbm.at[t, pl.ds(rows, half)], od_sems.at[t])

    def send_dkv(t):
        return pltpu.make_async_copy(dkv_ref.at[t], z_hbm.at[t, pl.ds(0, rows)], dkv_sems.at[t])

    query_blocks(
        pattern_ref, valid_ref, start_ref, kv_ref, qg_ref, acc_ref, od_ref, both_ref, pd_ref,
        send_od, chunk=1, ready=copies[1].wait, **sizes,
    )
    low = lax.broadcasted_iota(jnp.int32, (rows, PAIR), 1) < HEAD_DIM

    def scaled(s):
        tile = acc_ref[pl.ds(pl.multiple_of(s * rows, rows), rows), :]
        return jnp.where(low, tile * score_scale, tile)

    for t in range(edge, shards - edge):
        dkv_ref[t] = scaled(edge + t).astype(dkv_ref.dtype)
        send_dkv(t).start()
    odd, above, end = odd_ref[0], edge + shards, shards - edge
    for s in range(edge):
        inner_rim_ref[s] = scaled((1 - odd) * above + s).astype(inner_rim_ref.dtype)
        outer_rim_ref[s] = scaled(odd * above + s).astype(outer_rim_ref.dtype)
        inner_own_ref[s] = scaled(edge + (1 - odd) * end + s)
        outer_own_ref[s] = scaled(edge + odd * end + s)
    for t in range(shards):
        send_od(t).wait()
    for t in range(edge, shards - edge):
        send_dkv(t).wait()


def cost(tokens, keys_num):
    work = tokens * keys_num * BLOCK
    return pl.CostEstimate(flops=12 * PAIR * work, transcendentals=work, bytes_accessed=16 << 20)


def first_half(pattern, valid_rows, start, odd, x, inner, outer, group=16, lines=16):
    keys_num = pattern.shape[0] * BLOCK // (x.shape[0] * inner.shape[1])
    shards, edge, rows = x.shape[0], inner.shape[0], inner.shape[1]
    half, ext = rows // 2, shards + 2 * edge
    smem = pl.BlockSpec(memory_space=pltpu.SMEM)
    hbm = pl.BlockSpec(memory_space=pltpu.HBM)
    vmem = pl.BlockSpec(memory_space=pltpu.VMEM)
    return pl.pallas_call(
        partial(first_kernel, keys_num=keys_num, group=group, lines=lines),
        out_shape=(
            pltpu.HBM((shards, half, PAIR), x.dtype),
            pltpu.HBM((ext * rows, PAIR), x.dtype),
            pltpu.HBM((ext * rows, PAIR), jnp.float32),
        ),
        in_specs=[smem, smem, smem, smem, hbm, vmem, vmem],
        out_specs=(hbm, hbm, hbm),
        scratch_shapes=[
            pltpu.VMEM((ext * rows, PAIR), x.dtype),
            pltpu.VMEM((ext * rows, PAIR), jnp.float32),
            pltpu.VMEM((shards, half, PAIR), x.dtype),
            pltpu.VMEM((shards, half, PAIR), x.dtype),
            pltpu.VMEM((group, PAIR, keys_num * BLOCK), jnp.float32),
            pltpu.VMEM((group, PAIR, keys_num * BLOCK), x.dtype),
            pltpu.SemaphoreType.DMA((ext + 1,)),
            pltpu.SemaphoreType.DMA((shards,)),
            pltpu.SemaphoreType.DMA((2,)),
        ],
        compiler_params=pltpu.CompilerParams(vmem_limit_bytes=32 << 20),
        cost_estimate=cost(shards * half, keys_num),
        name="first_half",
    )(pattern, valid_rows, start, odd, off_chip(x), on_chip(inner), on_chip(outer))


def second_half(pattern, valid_rows, start, odd, x, kv, acc, edge, group=32, lines=16):
    shards, half = x.shape[:2]
    rows = 2 * half
    keys_num = pattern.shape[0] * BLOCK // (shards * rows)
    smem = pl.BlockSpec(memory_space=pltpu.SMEM)
    hbm = pl.BlockSpec(memory_space=pltpu.HBM)
    vmem = pl.BlockSpec(memory_space=pltpu.VMEM)
    face = (edge, rows, PAIR)
    return pl.pallas_call(
        partial(second_kernel, keys_num=keys_num, group=group, lines=lines),
        out_shape=(pltpu.HBM((shards, rows + half, PAIR), x.dtype),)
        + (pltpu.VMEM(face, jnp.float32),) * 2
        + (pltpu.VMEM(face, x.dtype),) * 2,
        in_specs=[smem, smem, smem, smem, vmem, hbm, hbm],
        out_specs=(hbm, vmem, vmem, vmem, vmem),
        scratch_shapes=[
            pltpu.VMEM(kv.shape, kv.dtype),
            pltpu.VMEM(acc.shape, acc.dtype),
            pltpu.VMEM((shards, half, PAIR), x.dtype),
            pltpu.VMEM((shards, rows, PAIR), x.dtype),
            pltpu.VMEM((group, PAIR, keys_num * BLOCK), jnp.float32),
            pltpu.VMEM((group, PAIR, keys_num * BLOCK), x.dtype),
            pltpu.SemaphoreType.DMA((2,)),
            pltpu.SemaphoreType.DMA((shards,)),
            pltpu.SemaphoreType.DMA((shards,)),
        ],
        compiler_params=pltpu.CompilerParams(vmem_limit_bytes=32 << 20),
        cost_estimate=cost(shards * half, keys_num),
        name="second_half",
    )(pattern, valid_rows, start, odd, on_chip(x), off_chip(kv), off_chip(acc))


def join_kernel(
    odd_ref, z_in, inner_ref, outer_ref, inner_rim_ref, outer_rim_ref, z_hbm, sum_ref, sems,
):
    edge, rows = inner_ref.shape[:2]
    odd = odd_ref[0]
    shards = z_hbm.shape[0]
    sum_ref[0] = (inner_ref[...] + inner_rim_ref[...].astype(jnp.float32)).astype(sum_ref.dtype)
    sum_ref[1] = (outer_ref[...] + outer_rim_ref[...].astype(jnp.float32)).astype(sum_ref.dtype)
    copies = [
        pltpu.make_async_copy(
            sum_ref.at[i], z_hbm.at[pl.ds(at, edge), pl.ds(0, rows)], sems.at[i]
        )
        for i, at in enumerate(((1 - odd) * (shards - edge), odd * (shards - edge)))
    ]
    for copy in copies:
        copy.start()
    for copy in copies:
        copy.wait()


def join_faces(odd, z, inner, outer, inner_rim, outer_rim):
    hbm = pl.BlockSpec(memory_space=pltpu.HBM)
    vmem = pl.BlockSpec(memory_space=pltpu.VMEM)
    return pl.pallas_call(
        join_kernel,
        out_shape=pltpu.HBM(z.shape, z.dtype),
        in_specs=[pl.BlockSpec(memory_space=pltpu.SMEM), hbm, vmem, vmem, vmem, vmem],
        out_specs=hbm,
        scratch_shapes=[pltpu.VMEM((2, *inner_rim.shape), z.dtype), pltpu.SemaphoreType.DMA((2,))],
        input_output_aliases={1: 0},
        compiler_params=pltpu.CompilerParams(vmem_limit_bytes=8 << 20),
        name="join_faces",
    )(odd, z, *(on_chip(a) for a in (inner, outer, inner_rim, outer_rim)))


def body(query, key, value, grad_out, pattern, valid_rows):
    def exchange(x):
        return lax.all_to_all(x, "seq", split_axis=0, concat_axis=0, tiled=True)

    size = lax.axis_size("slab")
    inside = [(i, j) for i in range(size) if 0 <= (j := i - 1 + 2 * (i % 2)) < size]
    outside = [(i, i ^ 1) for i in range(size) if i ^ 1 < size]
    odd = ((lax.axis_index("slab") + 1) % 2).astype(jnp.int32).reshape(1)
    rows = query.shape[0]
    edge = FACE * BLOCK // rows
    half, chunk = rows // 2, rows // CHUNKS
    one, two = pack_heads(key, value, query, grad_out)
    one = exchange(one)
    inner, outer = take_faces(odd, one, edge, rows)
    inner = lax.ppermute(inner, "slab", inside)
    outer = lax.ppermute(outer, "slab", outside)
    two = exchange(two)
    start = (lax.axis_index("slab") * pattern.shape[0] - FACE).astype(jnp.int32).reshape(1)
    scalars = (pattern.reshape(-1), valid_rows, start, odd)
    od, kv, acc = first_half(*scalars, one, inner, outer)
    od = exchange(od)
    z, inner, outer, inner_rim, outer_rim = second_half(*scalars, two, kv, acc, edge)
    inner_rim = lax.ppermute(inner_rim, "slab", inside)
    outer_rim = lax.ppermute(outer_rim, "slab", outside)
    done = unpack_heads(od, rows, chunks(0, 0, half, 0, chunk), 2, "unpack_first")
    z, *done = lax.optimization_barrier((z, *done))
    z = exchange(join_faces(odd, z, inner, outer, inner_rim, outer_rim))
    jobs = chunks(0, 0, rows, 0, chunk) + chunks(2, half, half, rows, chunk)
    grad_key, grad_value, grad_query, attn_out = unpack_heads(
        z, rows, jobs, 4, "unpack_second", into=done
    )
    return (attn_out, grad_query, grad_key, grad_value)


def solution(mesh):
    rows = P(("slab", "seq"), None)
    return jax.shard_map(
        body,
        mesh=mesh,
        in_specs=(rows, rows, rows, rows, P("slab", None), P()),
        out_specs=(rows, rows, rows, rows),
        check_vma=False,
    )
```
